256 devices in a mesh: lat: 16 (over z, y_hi), lon: 16 (over y_lo, x, core).
Axes of the slice: x: 4, y: 4 (y_hi: 2, y_lo: 2; y = y_hi * 2 + y_lo), z: 8, core: 2. Of those that a mesh axis runs over, the one named last changes fastest.
Arguments:
- fields: bfloat16 [69, 256, 2048], P(None, 'lat', 'lon'), may hold values from -6 to 6
- enc_kernel: bfloat16 [3, 3, 256, 69], replicated, may hold values from -0.25 to 0.25
- gen_kernel: bfloat16 [3, 3, 69, 256], replicated, may hold values from -0.125 to 0.125
- recon_grad: bfloat16 [69, 256, 2048], P(None, 'lat', 'lon'), may hold values from -6 to 6
Outputs:
- rebuilt: bfloat16 [69, 256, 2048], P(None, 'lat', 'lon')
- feat_grad: bfloat16 [256, 256, 2048], P(None, 'lat', 'lon')
- enc_grad: float32 [3, 3, 256, 69], replicated
- gen_grad: float32 [3, 3, 69, 256], replicated
The draws below stay inside these ranges and needn't reach their ends.
All inputs are finite; a program needn't handle non-finite values.
Results may differ from the reference program's by a relative error of at most 0.0085.
Values may be sent and summed in bfloat16 or wider, within the bound.
No kernel may reach another device: no remote copies, remote signals or barrier semaphores. Data moves between devices by JAX's collectives and lax.ppermute only.
A program may use at most 64 MiB of HBM per device.

```python
import jax
import jax.numpy as jnp
from jax import lax

CIN = 69
CH = 256
LAT = 256
LON = 2048


def block_scale(key, extent, pieces, least, top_value):
    gain, own = 1.0, jax.random.fold_in(key, 6)
    for dim, parts in pieces:
        heights = jnp.exp(jax.random.uniform(jax.random.fold_in(own, dim), (parts,), jnp.float32, least / len(pieces), top_value / len(pieces)))
        gain = gain * jnp.repeat(heights, extent[dim] // parts).reshape([-1 if axis == dim else 1 for axis in range(len(extent))])
    return gain


def normal_values(key, extent, scale, most, cuts=(), dtype=jnp.bfloat16):
    gain = block_scale(key, extent, cuts, -0.22, 0.18) if cuts else 1.0
    drawn = jax.random.normal(key, extent, jnp.float32) * scale * gain
    return jnp.minimum(jnp.maximum(drawn, -most), most).astype(dtype)


def setup_inputs(seed: int = 0) -> dict:
    key_list = jax.random.split(jax.random.key(seed), 5)
    return {
        "fields": normal_values(key_list[0], (CIN, LAT, LON), 1.0, 6.0, ((1, 16), (2, 16))),
        "enc_kernel": normal_values(key_list[1], (3, 3, CH, CIN), (9 * CIN) ** -0.5, 0.25),
        "gen_kernel": normal_values(key_list[2], (3, 3, CIN, CH), (9 * CH) ** -0.5, 0.125),
        "recon_grad": normal_values(key_list[3], (CIN, LAT, LON), 1.0, 6.0, ((1, 16), (2, 16))),
    }


def pole_pad(source):
    lon_cells = source.shape[2]
    upper = jnp.roll(source[:, :1], lon_cells // 2, axis=2)
    lower = jnp.roll(source[:, -1:], lon_cells // 2, axis=2)
    stacked = jnp.concatenate([upper, source, lower], axis=1)
    return jnp.concatenate([stacked[:, :, -1:], stacked, stacked[:, :, :1]], axis=2)

def convolve(padded, kernel, height, width):
    running = jnp.zeros((kernel.shape[2], height * width), jnp.float32)
    for row_tap in range(3):
        for col_tap in range(3):
            section = padded[:, row_tap:row_tap + height, col_tap:col_tap + width].reshape(padded.shape[0], height * width)
            running = running + jnp.dot(kernel[row_tap, col_tap], section, preferred_element_type=jnp.float32)
    return running.reshape(kernel.shape[2], height, width)

def weight_grad(cotangent, padded, height, width):
    flat_cot = cotangent.reshape(cotangent.shape[0], height * width)
    taps = []
    for row_tap in range(3):
        row_list = []
        for col_tap in range(3):
            section = padded[:, row_tap:row_tap + height, col_tap:col_tap + width].reshape(padded.shape[0], height * width)
            row_list.append(lax.dot_general(flat_cot, section, (((1,), (1,)), ((), ())), preferred_element_type=jnp.float32))
        taps.append(jnp.stack(row_list))
    return jnp.stack(taps)

def adjoint_conv(cotangent, kernel, height, width):
    flat_cot = cotangent.reshape(cotangent.shape[0], height * width)
    spread = jnp.zeros((kernel.shape[3], height + 2, width + 2), jnp.float32)
    for row_tap in range(3):
        for col_tap in range(3):
            product = lax.dot_general(kernel[row_tap, col_tap], flat_cot, (((0,), (0,)), ((), ())), preferred_element_type=jnp.float32)
            spread = spread.at[:, row_tap:row_tap + height, col_tap:col_tap + width].add(product.reshape(kernel.shape[3], height, width))
    folded = spread[:, :, 1:-1]
    folded = folded.at[:, :, -1].add(spread[:, :, 0])
    folded = folded.at[:, :, 0].add(spread[:, :, -1])
    inner = folded[:, 1:-1]
    inner = inner.at[:, 0].add(jnp.roll(folded[:, 0], width // 2, axis=1))
    inner = inner.at[:, -1].add(jnp.roll(folded[:, -1], width // 2, axis=1))
    return inner

def reference(fields, enc_kernel, gen_kernel, recon_grad):
    height = fields.shape[1]
    width = fields.shape[2]
    padded_in = pole_pad(fields)
    pre_act = convolve(padded_in, enc_kernel, height, width)
    hidden = jax.nn.silu(pre_act).astype(jnp.bfloat16)
    padded_hid = pole_pad(hidden)
    rebuilt = convolve(padded_hid, gen_kernel, height, width).astype(jnp.bfloat16)
    feat_grad = adjoint_conv(recon_grad, gen_kernel, height, width).astype(jnp.bfloat16)
    logistic = jax.nn.sigmoid(pre_act)
    pre_grad = (feat_grad.astype(jnp.float32) * logistic * (1.0 + pre_act * (1.0 - logistic))).astype(jnp.bfloat16)
    norm_scale = 1.0 / jnp.sqrt(jnp.float32(LAT * LON))
    gen_grad = weight_grad(recon_grad, padded_hid, height, width) * norm_scale
    enc_grad = weight_grad(pre_grad, padded_in, height, width) * norm_scale
    return (rebuilt, feat_grad, enc_grad, gen_grad)
```

```python
import jax
import jax.numpy as jnp
from jax import lax
from jax.sharding import Mesh
from jax.sharding import PartitionSpec as P


def extended(cells, sides, width, closed):
    for axis, dim in sides:
        count = lax.axis_size(axis)
        ends = count if closed else count - 1
        head = lax.slice_in_dim(cells, 0, width, axis=dim)
        tail = lax.slice_in_dim(cells, cells.shape[dim] - width, cells.shape[dim], axis=dim)
        cells = jnp.concatenate(
            [
                lax.ppermute(tail, axis, [(i, (i + 1) % count) for i in range(ends)]),
                cells,
                lax.ppermute(head, axis, [((i + 1) % count, i) for i in range(ends)]),
            ],
            axis=dim,
        )
    return cells


def from_behind(value, axis, steps):
    count = lax.axis_size(axis)
    pairs = [(source, (source + steps) % count) for source in range(count)]
    return lax.ppermute(value, axis, pairs)


def face_pad(source):
    lon_count = lax.axis_size(LON)
    widened = extended(source, ((LON, 2),), 1, True)
    edge_rows = jnp.concatenate([widened[:, :1], widened[:, -1:]], axis=1)
    pole_rows = from_behind(edge_rows, LON, lon_count // 2)
    plain_pad = extended(widened, ((LAT, 1),), 1, False)
    result = (plain_pad, pole_rows)
    return result


def with_poles(plain_pad, pole_rows):
    lat_index = lax.axis_index(LAT)
    lat_count = lax.axis_size(LAT)
    upper = jnp.where(lat_index == 0, pole_rows[:, :1], plain_pad[:, :1])
    lower = jnp.where(lat_index == lat_count - 1, pole_rows[:, 1:], plain_pad[:, -1:])
    return jnp.concatenate([upper, plain_pad[:, 1:-1], lower], axis=1)


def convolve(padded, kernel, height, width):
    running = None
    for row_tap in range(3):
        for col_tap in range(3):
            section = padded[:, row_tap : row_tap + height, col_tap : col_tap + width].reshape(
                padded.shape[0], height * width
            )
            product = jnp.dot(kernel[row_tap, col_tap], section, preferred_element_type=jnp.float32)
            running = product if running is None else running + product
    return running.reshape(kernel.shape[2], height, width)


def adjoint_conv(padded, kernel, height, width):
    running = None
    for row_tap in range(3):
        for col_tap in range(3):
            section = padded[
                :, 2 - row_tap : 2 - row_tap + height, 2 - col_tap : 2 - col_tap + width
            ].reshape(padded.shape[0], height * width)
            product = lax.dot_general(
                kernel[row_tap, col_tap],
                section,
                (((0,), (0,)), ((), ())),
                preferred_element_type=jnp.float32,
            )
            running = product if running is None else running + product
    return running.reshape(kernel.shape[3], height, width)


def pole_terms(pole_rows, kernel, width):
    terms = []
    for which, row_tap in ((0, 0), (1, 2)):
        running = None
        for col_tap in range(3):
            section = pole_rows[:, which, 2 - col_tap : 2 - col_tap + width]
            product = lax.dot_general(
                kernel[row_tap, col_tap],
                section,
                (((0,), (0,)), ((), ())),
                preferred_element_type=jnp.float32,
            )
            running = product if running is None else running + product
        terms.append(running)
    return (terms[0], terms[1])


def weight_grad(cotangent, padded, height, width):
    flat_cot = cotangent.reshape(cotangent.shape[0], height * width)
    taps = []
    for row_tap in range(3):
        row_list = []
        for col_tap in range(3):
            section = padded[:, row_tap : row_tap + height, col_tap : col_tap + width].reshape(
                padded.shape[0], height * width
            )
            row_list.append(
                lax.dot_general(
                    flat_cot, section, (((1,), (1,)), ((), ())), preferred_element_type=jnp.float32
                )
            )
        taps.append(jnp.stack(row_list))
    return jnp.stack(taps)


CHIPS = ("z", "y_hi", "y_lo", "x")
LAT = ("z", "y_hi")
LON = ("y_lo", "x", "core")


def swap_cores(value):
    return lax.ppermute(value, "core", [(0, 1), (1, 0)])


def sum_grads(enc_part, gen_part):
    chips = lax.axis_size(CHIPS)
    first = lax.axis_index("core") == 0
    enc_part = jnp.swapaxes(enc_part, 2, 3)
    shape = gen_part.shape
    lanes = 128
    cells = enc_part.size
    rows = -(-cells // (chips * 2 * lanes))
    kept = jnp.where(first, gen_part, enc_part)
    sent = jnp.where(first, enc_part, gen_part).astype(jnp.bfloat16)
    half = (kept + swap_cores(sent).astype(jnp.float32)).astype(jnp.bfloat16)
    half = jnp.pad(half.reshape(-1), (0, chips * rows * 2 * lanes - cells))
    pieces = lax.all_to_all(half.reshape(chips, rows, 2, lanes), CHIPS, 0, 0, tiled=True)
    total = jnp.sum(pieces.astype(jnp.float32), axis=0).astype(jnp.bfloat16)
    spread = jnp.broadcast_to(total[None], pieces.shape)
    whole = lax.all_to_all(spread, CHIPS, 0, 0, tiled=True).reshape(-1)[:cells].reshape(shape)
    other = swap_cores(whole)
    gen_sum = jnp.where(first, whole, other).astype(jnp.float32)
    enc_sum = jnp.where(first, other, whole).astype(jnp.float32)
    return jnp.swapaxes(enc_sum, 2, 3), gen_sum


def on_device(fields, enc_kernel, gen_kernel, recon_grad):
    height = fields.shape[1]
    width = fields.shape[2]
    lat_index = lax.axis_index(LAT)
    lat_count = lax.axis_size(LAT)
    lon_count = lax.axis_size(LON)
    plain_in, pole_in = face_pad(fields)
    plain_cot, pole_cot = face_pad(recon_grad)
    padded_in = with_poles(plain_in, pole_in)
    pre_act = convolve(padded_in, enc_kernel, height, width)
    hidden = jax.nn.silu(pre_act).astype(jnp.bfloat16)
    plain_hid, pole_hid = face_pad(hidden)
    padded_hid = with_poles(plain_hid, pole_hid)
    rebuilt = convolve(padded_hid, gen_kernel, height, width).astype(jnp.bfloat16)
    feat_f32 = adjoint_conv(plain_cot, gen_kernel, height, width)
    upper_term, lower_term = pole_terms(pole_cot, gen_kernel, width)
    feat_f32 = feat_f32.at[:, 0].add(jnp.where(lat_index == 0, upper_term, 0.0))
    feat_f32 = feat_f32.at[:, -1].add(jnp.where(lat_index == lat_count - 1, lower_term, 0.0))
    feat_grad = feat_f32.astype(jnp.bfloat16)
    logistic = jax.nn.sigmoid(pre_act)
    pre_grad = (
        feat_grad.astype(jnp.float32) * logistic * (1.0 + pre_act * (1.0 - logistic))
    ).astype(jnp.bfloat16)
    gen_part = weight_grad(recon_grad, padded_hid, height, width)
    enc_part = weight_grad(pre_grad, padded_in, height, width)
    enc_sum, gen_sum = sum_grads(enc_part, gen_part)
    norm_scale = 1.0 / jnp.sqrt(jnp.float32(height * lat_count * width * lon_count))
    return (rebuilt, feat_grad, enc_sum * norm_scale, gen_sum * norm_scale)


def solution(mesh):
    lat_count, lon_count = mesh.shape["lat"], mesh.shape["lon"]
    fine = Mesh(mesh.devices.reshape(lat_count // 2, 2, 2, lon_count // 4, 2), LAT + LON)
    return jax.shard_map(
        on_device,
        mesh=fine,
        in_specs=(P(None, LAT, LON), P(), P(), P(None, LAT, LON)),
        out_specs=(P(None, LAT, LON), P(None, LAT, LON), P(), P()),
        check_vma=False,
    )
```

```python
import functools

import jax
import jax.numpy as jnp
from jax import lax
from jax.experimental import pallas as pl
from jax.experimental.pallas import tpu as pltpu
from jax.sharding import Mesh
from jax.sharding import PartitionSpec as P

CHIPS = ("z", "y_hi", "y_lo", "x")
LAT = ("z", "y_hi")
LON = ("y_lo", "x", "core")

LANES = 128
ROWS = 16
DEEP = 80
BAND = 3 * DEEP
TAPS = 3 * BAND
PACK = 640
F32 = jnp.float32
BF16 = jnp.bfloat16
NT = (((1,), (1,)), ((), ()))
TN = (((0,), (0,)), ((), ()))
FULL = pl.BlockSpec(memory_space=pltpu.VMEM)
FLAGS = pl.BlockSpec(memory_space=pltpu.SMEM)


def lane_of(shape):
    return lax.broadcasted_iota(jnp.int32, shape, len(shape) - 1)


def dot(a, b, dims=(((1,), (0,)), ((), ()))):
    return lax.dot_general(a, b, dims, preferred_element_type=F32)


def call(kernel, outs, cost, scratch=(), limit=48):
    return functools.partial(
        pl.pallas_call,
        kernel,
        out_shape=outs,
        scratch_shapes=list(scratch),
        compiler_params=pltpu.CompilerParams(vmem_limit_bytes=limit << 20),
        cost_estimate=pl.CostEstimate(flops=cost, bytes_accessed=cost // 500, transcendentals=0),
    )


def pick(row, lane):
    rows = lax.broadcasted_iota(jnp.int32, (8, LANES), 0)
    lanes = lax.broadcasted_iota(jnp.int32, (8, LANES), 1)
    return (rows == row) & (lanes == lane)


def picks(pairs):
    hot = pick(*pairs[0])
    for pair in pairs[1:]:
        hot = hot | pick(*pair)
    return jnp.where(hot, 1.0, 0.0).astype(BF16)


def columns_kernel(x_ref, r_ref, east_ref, west_ref):
    x = x_ref[...].reshape(ROWS * DEEP, LANES)
    r = r_ref[...].reshape(ROWS * DEEP, LANES)
    east = dot(picks([(0, 126), (1, 127)]), x, NT) + dot(picks([(2, 127)]), r, NT)
    west = dot(picks([(0, 0), (1, 1)]), x, NT) + dot(picks([(2, 0)]), r, NT)
    east_ref[...] = east.astype(BF16)
    west_ref[...] = west.astype(BF16)


def rows_kernel(flags_ref, x_ref, r_ref, east_ref, west_ref, hx_ref, hr_ref, a_ref, b_ref):
    low = flags_ref[3] == 1
    left = east_ref[...].astype(F32).T.astype(BF16)
    right = west_ref[...].astype(F32).T.astype(BF16)
    hx = dot(left, picks([(0, 126), (1, 127)])) + dot(right, picks([(0, 0), (1, 1)]))
    hr = dot(left, picks([(2, 127)])) + dot(right, picks([(2, 0)]))
    hx_ref[...] = hx.astype(BF16).reshape(ROWS, DEEP, LANES)
    hr_ref[...] = hr.astype(BF16).reshape(ROWS, DEEP, LANES)
    top = (x_ref[0], x_ref[1], r_ref[0], hx_ref[0], hx_ref[1], hr_ref[0])
    end = ROWS - 1
    bottom = (x_ref[end], x_ref[end - 1], r_ref[end], hx_ref[end], hx_ref[end - 1], hr_ref[end])
    for k in range(6):
        t, b = top[k].astype(F32), bottom[k].astype(F32)
        a_ref[k] = jnp.where(low, b, t).astype(BF16)
        b_ref[k] = jnp.where(low, t, b).astype(BF16)


def shifts(x, h):
    lane = lane_of(x.shape)
    left = pltpu.roll(jnp.where(lane == LANES - 1, h, x), 1, 1)
    right = pltpu.roll(jnp.where(lane == 0, h, x), LANES - 1, 1)
    return left, right


def main_kernel(
    flags_ref, x_ref, r_ref, hx_ref, hr_ref, pa_ref, pb_ref, we_ref, gt_ref,
    feat_ref, hid_ref, strip_ref, sent_ref, kept_ref,
    f_s, r_s, pole_s, u_s, fx_s, acc_s, pack_s,
):
    north, south = flags_ref[0] == 1, flags_ref[1] == 1
    core, low = flags_ref[2], flags_ref[3] == 1
    lane = lane_of((DEEP, LANES))
    u_s[...] = jnp.zeros_like(u_s)

    def put_field(slot, x, h):
        left, right = shifts(x, h)
        f_s[slot, :DEEP, :] = left.astype(BF16)
        f_s[slot, DEEP : 2 * DEEP, :] = x.astype(BF16)
        f_s[slot, 2 * DEEP :, :] = right.astype(BF16)
        spot = 2 * slot
        hit = (lane == spot) | (lane == spot + 1)
        sides = (
            (jnp.where(lane == LANES - 1, x, h), spot + 2),
            (h, spot + 1),
            (jnp.where(lane == 0, x, h), spot),
        )
        for tap, (plane, turn) in enumerate(sides):
            turned = pltpu.roll(plane, turn, 1)
            rows = pl.ds(tap * DEEP, DEEP)
            u_s[rows, :] = jnp.where(hit, turned, u_s[rows, :])

    def put_cot(ref, slot, x, h):
        left, right = shifts(x, h)
        ref[slot, :DEEP, :] = right.astype(BF16)
        ref[slot, DEEP : 2 * DEEP, :] = x.astype(BF16)
        ref[slot, 2 * DEEP :, :] = left.astype(BF16)

    def fill(row, carry):
        put_field(row + 2, x_ref[row].astype(F32), hx_ref[row].astype(F32))
        put_cot(r_s, ROWS - row, r_ref[row].astype(F32), hr_ref[row].astype(F32))
        return carry

    lax.fori_loop(0, ROWS, fill, 0)
    pa = [pa_ref[k].astype(F32) for k in range(6)]
    pb = [pb_ref[k].astype(F32) for k in range(6)]
    up = [jnp.where(low, a, b) for a, b in zip(pa, pb)]
    down = [jnp.where(low, b, a) for a, b in zip(pa, pb)]
    put_field(1, up[0], up[3])
    put_field(0, up[1], up[4])
    put_field(ROWS + 2, down[0], down[3])
    put_field(ROWS + 3, down[1], down[4])
    put_cot(r_s, ROWS + 1, jnp.where(north, 0.0, up[2]), jnp.where(north, 0.0, up[5]))
    put_cot(r_s, 0, jnp.where(south, 0.0, down[2]), jnp.where(south, 0.0, down[5]))
    put_cot(pole_s, 0, jnp.where(north, up[2], 0.0), jnp.where(north, up[5], 0.0))
    put_cot(pole_s, 1, jnp.where(south, down[2], 0.0), jnp.where(south, down[5], 0.0))

    we, gt = we_ref[...], gt_ref[...]

    def band(slot):
        return f_s[slot].astype(F32)

    def swapped(flag, first, last):
        return jnp.where(flag, last, first).astype(BF16), jnp.where(flag, first, last).astype(BF16)

    def silu(v):
        return v * (1.0 / (1.0 + jnp.exp(-v)))

    n0, n2 = swapped(north, band(0), band(2))
    s0, s2 = swapped(south, band(ROWS + 1), band(ROWS + 3))
    ring = jnp.concatenate(
        [
            jnp.concatenate([n0, f_s[1], n2], axis=0),
            jnp.concatenate([s0, f_s[ROWS + 2], s2], axis=0),
        ],
        axis=1,
    )
    halo = silu(dot(we, ring)).astype(BF16)
    hid_ref[0] = halo[:, :LANES]
    hid_ref[ROWS + 1] = halo[:, LANES:]

    u = u_s[...]
    u2 = pltpu.roll(u, LANES - 2, 1)
    u4 = pltpu.roll(u, LANES - 4, 1)
    wide = lane_of(u.shape)
    last = 2 * (ROWS + 1)
    flip = (north & (wide < 2)) | (south & ((wide == last) | (wide == last + 1)))
    strip = jnp.concatenate(
        [jnp.where(flip, u4, u).astype(BF16), u2.astype(BF16), jnp.where(flip, u, u4).astype(BF16)],
        axis=0,
    )
    strip_ref[...] = silu(dot(we, strip)).astype(BF16)

    fx_s[:, :LANES] = dot(gt[:, :BAND], pole_s[0])
    fx_s[:, LANES:] = dot(gt[:, 2 * BAND :], pole_s[1])
    acc_s[...] = jnp.zeros_like(acc_s)

    def two(ref, first, second):
        a = ref[pl.ds(first, 3)].reshape(TAPS, LANES)
        b = ref[pl.ds(second, 3)].reshape(TAPS, LANES)
        return jnp.concatenate([a, b], axis=1)

    half = lane_of(fx_s.shape) < LANES

    def step(pair, carry):
        f2 = two(f_s, 2 * pair + 1, 2 * pair + 2)
        r2 = two(r_s, ROWS - 1 - 2 * pair, ROWS - 2 - 2 * pair)
        pre = dot(we_ref[...], f2)
        gate = 1.0 / (1.0 + jnp.exp(-pre))
        hid = (pre * gate).astype(BF16)
        edge = ((pair == 0) & half) | ((pair == ROWS // 2 - 1) & ~half)
        feat = (dot(gt_ref[...], r2) + jnp.where(edge, fx_s[...], 0.0)).astype(BF16)
        feat_ref[2 * pair] = feat[:, :LANES]
        feat_ref[2 * pair + 1] = feat[:, LANES:]
        hid_ref[2 * pair + 1] = hid[:, :LANES]
        hid_ref[2 * pair + 2] = hid[:, LANES:]
        back = (feat.astype(F32) * gate * (1.0 + pre * (1.0 - gate))).astype(BF16)
        acc_s[0] += dot(r2, hid, NT)
        acc_s[1] += dot(f2, back, NT)
        return carry

    lax.fori_loop(0, ROWS // 2, step, 0)
    acc_s[0, :BAND, :] += dot(pole_s[0], hid_ref[1], NT)
    acc_s[0, 2 * BAND :, :] += dot(pole_s[1], hid_ref[ROWS], NT)

    def pack(which, out_ref):
        for tap in range(9):
            pack_s[69 * tap : 69 * tap + 69, :] = acc_s[which, DEEP * tap : DEEP * tap + 69, :]
        pack_s[621:, :] = jnp.zeros((pack_s.shape[0] - 621, pack_s.shape[1]), F32)
        out_ref[:PACK, :] = pack_s[:PACK, :LANES].astype(out_ref.dtype)
        out_ref[PACK:, :] = pack_s[:PACK, LANES:].astype(out_ref.dtype)

    pack(1 - core, sent_ref)
    pack(core, kept_ref)


def rebuilt_kernel(hid_ref, strip_ref, ga_ref, out_ref, z_s, t_s):
    ga = ga_ref[...]
    zs = dot(ga, strip_ref[...])
    t0 = zs[:DEEP]
    t2 = zs[2 * DEEP : BAND]
    for a in (1, 2):
        t0 = t0 + pltpu.roll(zs[a * BAND : a * BAND + DEEP], LANES - 2 * a, 1)
        t2 = t2 + pltpu.roll(zs[a * BAND + 2 * DEEP : (a + 1) * BAND], LANES - 2 * a, 1)
    lane = lane_of((DEEP, LANES))
    even = lax.rem(lane, 2) == 0
    t_s[...] = jnp.where(even, pltpu.roll(t2, LANES - 1, 1), pltpu.roll(t0, 1, 1))

    def fill(pair, carry):
        z = dot(ga, jnp.concatenate([hid_ref[2 * pair], hid_ref[2 * pair + 1]], axis=1))
        z_s[2 * pair] = z[:, :LANES]
        z_s[2 * pair + 1] = z[:, LANES:]
        return carry

    lax.fori_loop(0, ROWS // 2 + 1, fill, 0)

    def emit(row, carry):
        sums = []
        for b in range(3):
            total = z_s[row, b * DEEP : (b + 1) * DEEP, :]
            for a in (1, 2):
                start = a * BAND + b * DEEP
                total = total + z_s[row + a, start : start + DEEP, :]
            sums.append(total)
        out = sums[1]
        out = out + jnp.where(lane == 0, 0.0, pltpu.roll(sums[0], 1, 1))
        out = out + jnp.where(lane == LANES - 1, 0.0, pltpu.roll(sums[2], LANES - 1, 1))
        side = pltpu.roll(t_s[...], LANES - 1 - 2 * row, 1)
        out = out + jnp.where((lane == 0) | (lane == LANES - 1), side, 0.0)
        out_ref[row] = out.astype(BF16)
        return carry

    lax.fori_loop(0, ROWS, emit, 0)


def total_kernel(pieces_ref, out_ref):
    count = pieces_ref.shape[0]
    group = count // 128
    rows = lax.broadcasted_iota(jnp.int32, (16, count), 0)
    cells = lax.broadcasted_iota(jnp.int32, (16, count), 1)
    hot = jnp.where(lax.rem(cells, group) == rows, 1.0, 0.0).astype(BF16)
    total = dot(hot, pieces_ref[...]).astype(BF16)
    out_ref[...] = dot(hot, total, TN).astype(BF16)


def final_kernel(norm, flags_ref, own_ref, other_ref, enc_ref, gen_ref, pack_s):
    first = flags_ref[2] == 0
    own, other = own_ref[...].astype(F32), other_ref[...].astype(F32)
    gen = jnp.where(first, own, other) * norm
    enc = jnp.where(first, other, own) * norm
    for value, out in ((gen, gen_ref), (enc, enc_ref)):
        pack_s[...] = value
        for tap in range(9):
            out[tap, :, :LANES] = pack_s[69 * tap : 69 * tap + 69, :]
            out[tap, :, LANES:] = pack_s[PACK + 69 * tap : PACK + 69 * tap + 69, :]


def swap_cores(value):
    return lax.ppermute(value, "core", [(0, 1), (1, 0)])


def planes(v):
    return jnp.pad(jnp.transpose(v, (1, 0, 2)), ((0, 0), (0, DEEP - v.shape[0]), (0, 0)))


def great_circles(lat_count, lon_count):
    pairs = []
    for la in range(lat_count):
        for lo in range(lon_count):
            if lo < lon_count // 2:
                to = (la + 1, lo) if la < lat_count - 1 else (la, lo + lon_count // 2)
            else:
                to = (la - 1, lo) if la > 0 else (la, lo - lon_count // 2)
            pairs.append((la * lon_count + lo, to[0] * lon_count + to[1]))
    return pairs, [(b, a) for a, b in pairs]


def on_device(fields, enc_kernel, gen_kernel, recon_grad):
    variables, height, width = fields.shape
    channels = gen_kernel.shape[3]
    lat_index, lat_count = lax.axis_index(LAT), lax.axis_size(LAT)
    lon_count = lax.axis_size(LON)
    chips = lax.axis_size(CHIPS)
    core = lax.axis_index("core")
    low = lax.axis_index("y_lo") == 0
    flags = jnp.stack(
        [
            (lat_index == 0).astype(jnp.int32),
            (lat_index == lat_count - 1).astype(jnp.int32),
            core.astype(jnp.int32),
            low.astype(jnp.int32),
        ]
    )
    pad = ((0, 0), (0, 0), (0, DEEP - variables), (0, 0))
    gen_rows = jnp.pad(gen_kernel, pad).reshape(TAPS, channels)
    enc_rows = jnp.pad(jnp.swapaxes(enc_kernel, 2, 3), pad).reshape(TAPS, channels)
    x, r = planes(fields), planes(recon_grad)

    plane = jax.ShapeDtypeStruct((ROWS, DEEP, LANES), BF16)
    side = jax.ShapeDtypeStruct((8, ROWS * DEEP), BF16)
    east, west = call(columns_kernel, (side, side), 10**7)(
        in_specs=[FULL] * 2, out_specs=(FULL, FULL)
    )(x, r)
    right = [(i, (i + 1) % lon_count) for i in range(lon_count)]
    left = [(b, a) for a, b in right]
    from_left = lax.ppermute(east, LON, right)
    from_right = lax.ppermute(west, LON, left)
    packet = jax.ShapeDtypeStruct((6, DEEP, LANES), BF16)
    hx, hr, pa, pb = call(rows_kernel, (plane, plane, packet, packet), 10**7)(
        in_specs=[FLAGS] + [FULL] * 4, out_specs=(FULL,) * 4
    )(flags, x, r, from_left, from_right)
    ahead, behind = great_circles(lat_count, lon_count)
    pa = lax.ppermute(pa, LAT + LON, ahead)
    pb = lax.ppermute(pb, LAT + LON, behind)

    packed = (2 * PACK, LANES)
    feat, hid, strip, sent, kept = call(
        main_kernel,
        (
            jax.ShapeDtypeStruct((ROWS, channels, LANES), BF16),
            jax.ShapeDtypeStruct((ROWS + 2, channels, LANES), BF16),
            jax.ShapeDtypeStruct((channels, LANES), BF16),
            jax.ShapeDtypeStruct(packed, BF16),
            jax.ShapeDtypeStruct(packed, F32),
        ),
        3 * 10**9,
        [
            pltpu.VMEM((ROWS + 4, BAND, LANES), BF16),
            pltpu.VMEM((ROWS + 2, BAND, LANES), BF16),
            pltpu.VMEM((2, BAND, LANES), BF16),
            pltpu.VMEM((BAND, LANES), F32),
            pltpu.VMEM((channels, 2 * LANES), F32),
            pltpu.VMEM((2, TAPS, channels), F32),
            pltpu.VMEM((PACK + 8, channels), F32),
        ],
    )(in_specs=[FLAGS] + [FULL] * 8, out_specs=(FULL,) * 5)(
        flags, x, r, hx, hr, pa, pb, enc_rows.T, gen_rows.T
    )
    rows = call(
        rebuilt_kernel,
        plane,
        10**9,
        [pltpu.VMEM((ROWS + 2, TAPS, LANES), F32), pltpu.VMEM((DEEP, LANES), F32)],
    )(in_specs=[FULL] * 3, out_specs=FULL)(hid, strip, gen_rows)
    rebuilt = jnp.transpose(rows[:, :variables], (1, 0, 2))
    feat_grad = jnp.transpose(feat, (1, 0, 2))

    half = (kept + swap_cores(sent).astype(F32)).astype(BF16)
    cut = (chips, 2 * PACK // chips // 2, 2, LANES)
    pieces = lax.all_to_all(half.reshape(cut), CHIPS, 0, 0, tiled=True).reshape(packed)
    spread = call(total_kernel, jax.ShapeDtypeStruct(packed, BF16), 10**7)(
        in_specs=[FULL], out_specs=FULL
    )(pieces)
    own = lax.all_to_all(spread.reshape(cut), CHIPS, 0, 0, tiled=True).reshape(packed)
    other = swap_cores(own)
    norm = (height * lat_count * width * lon_count) ** -0.5
    grad = jax.ShapeDtypeStruct((9, variables, channels), F32)
    enc, gen = call(
        functools.partial(final_kernel, norm), (grad, grad), 10**7, [pltpu.VMEM(packed, F32)]
    )(in_specs=[FLAGS, FULL, FULL], out_specs=(FULL, FULL))(flags, own, other)
    shape = (3, 3, variables, channels)
    return (rebuilt, feat_grad, jnp.swapaxes(enc.reshape(shape), 2, 3), gen.reshape(shape))


def solution(mesh):
    lat_count, lon_count = mesh.shape["lat"], mesh.shape["lon"]
    fine = Mesh(mesh.devices.reshape(lat_count // 2, 2, 2, lon_count // 4, 2), LAT + LON)
    return jax.shard_map(
        on_device,
        mesh=fine,
        in_specs=(P(None, LAT, LON), P(), P(), P(None, LAT, LON)),
        out_specs=(P(None, LAT, LON), P(None, LAT, LON), P(), P()),
        check_vma=False,
    )
```

```python
import functools

import jax
import jax.numpy as jnp
from jax import lax
from jax.experimental import pallas as pl
from jax.experimental.pallas import tpu as pltpu
from jax.sharding import Mesh
from jax.sharding import PartitionSpec as P

FACE = ("y_hi", "y_lo", "x")
LAT = ("z", "y_hi")
LON = ("y_lo", "x", "core")

LANES = 128
ROWS = 16
DEEP = 80
SENT = 72
BAND = 3 * DEEP
TAPS = 3 * BAND
PACK = 640
F32 = jnp.float32
BF16 = jnp.bfloat16
NT = (((1,), (1,)), ((), ()))
TN = (((0,), (0,)), ((), ()))
FULL = pl.BlockSpec(memory_space=pltpu.VMEM)
FLAGS = pl.BlockSpec(memory_space=pltpu.SMEM)


def lane_of(shape):
    return lax.broadcasted_iota(jnp.int32, shape, len(shape) - 1)


def dot(a, b, dims=(((1,), (0,)), ((), ()))):
    return lax.dot_general(a, b, dims, preferred_element_type=F32)


def call(kernel, outs, cost, scratch=(), limit=8):
    return functools.partial(
        pl.pallas_call,
        kernel,
        out_shape=outs,
        scratch_shapes=list(scratch),
        compiler_params=pltpu.CompilerParams(vmem_limit_bytes=limit << 20),
        cost_estimate=pl.CostEstimate(flops=cost, bytes_accessed=cost // 500, transcendentals=0),
    )


def pick(row, lane):
    rows = lax.broadcasted_iota(jnp.int32, (8, LANES), 0)
    lanes = lax.broadcasted_iota(jnp.int32, (8, LANES), 1)
    return (rows == row) & (lanes == lane)


def picks(pairs):
    hot = pick(*pairs[0])
    for pair in pairs[1:]:
        hot = hot | pick(*pair)
    return jnp.where(hot, 1.0, 0.0).astype(BF16)


def columns_kernel(fields_ref, cot_ref, x_ref, r_ref, east_ref, west_ref, raw_s):
    for source, target in ((fields_ref, x_ref), (cot_ref, r_ref)):
        size = source.shape[0] * ROWS
        raw_s[:size, :] = source[...].astype(F32).reshape(size, LANES)
        raw_s[size:, :] = jnp.zeros((raw_s.shape[0] - size, LANES), F32)
        for row in range(ROWS):
            target[row] = raw_s[pl.ds(row, DEEP, stride=ROWS), :].astype(BF16)
    x = x_ref[...].reshape(ROWS * DEEP, LANES)
    r = r_ref[...].reshape(ROWS * DEEP, LANES)
    east = dot(picks([(0, 126), (1, 127)]), x, NT) + dot(picks([(2, 127)]), r, NT)
    west = dot(picks([(0, 0), (1, 1)]), x, NT) + dot(picks([(2, 0)]), r, NT)
    east_ref[...] = east.astype(BF16)
    west_ref[...] = west.astype(BF16)


def rows_kernel(flags_ref, x_ref, r_ref, east_ref, west_ref, hx_ref, hr_ref, a_ref, b_ref):
    low = flags_ref[3] == 1
    left = east_ref[...].astype(F32).T.astype(BF16)
    right = west_ref[...].astype(F32).T.astype(BF16)
    hx = dot(left, picks([(0, 126), (1, 127)])) + dot(right, picks([(0, 0), (1, 1)]))
    hr = dot(left, picks([(2, 127)])) + dot(right, picks([(2, 0)]))
    hx_ref[...] = hx.astype(BF16).reshape(ROWS, DEEP, LANES)
    hr_ref[...] = hr.astype(BF16).reshape(ROWS, DEEP, LANES)

    def packet(edge, inner):
        own = [x_ref[edge].astype(F32), x_ref[inner].astype(F32), r_ref[edge].astype(F32)]
        sides = hx_ref[edge].astype(F32) + pltpu.roll(hx_ref[inner].astype(F32), 4, 1)
        return own + [sides + pltpu.roll(hr_ref[edge].astype(F32), 8, 1)]

    top, bottom = packet(0, 1), packet(ROWS - 1, ROWS - 2)
    for k in range(4):
        t, b = top[k][:SENT], bottom[k][:SENT]
        a_ref[k] = jnp.where(low, b, t).astype(BF16)
        b_ref[k] = jnp.where(low, t, b).astype(BF16)


def shifts(x, h):
    lane = lane_of(x.shape)
    left = pltpu.roll(jnp.where(lane == LANES - 1, h, x), 1, 1)
    right = pltpu.roll(jnp.where(lane == 0, h, x), LANES - 1, 1)
    return left, right


def main_kernel(
    flags_ref, x_ref, r_ref, hx_ref, hr_ref, pa_ref, pb_ref, we_ref, gt_ref,
    feat_ref, hid_ref, strip_ref, sent_ref, kept_ref,
    f_s, r_s, pole_s, u_s, fx_s, acc_s, pack_s,
):
    north, south = flags_ref[0] == 1, flags_ref[1] == 1
    core, low = flags_ref[2], flags_ref[3] == 1
    lane = lane_of((DEEP, LANES))
    u_s[...] = jnp.zeros_like(u_s)

    def put_field(slot, x, h):
        left, right = shifts(x, h)
        f_s[slot, :DEEP, :] = left.astype(BF16)
        f_s[slot, DEEP : 2 * DEEP, :] = x.astype(BF16)
        f_s[slot, 2 * DEEP :, :] = right.astype(BF16)
        spot = 2 * slot
        hit = (lane == spot) | (lane == spot + 1)
        sides = (
            (jnp.where(lane == LANES - 1, x, h), spot + 2),
            (h, spot + 1),
            (jnp.where(lane == 0, x, h), spot),
        )
        for tap, (plane, turn) in enumerate(sides):
            turned = pltpu.roll(plane, turn, 1)
            rows = pl.ds(tap * DEEP, DEEP)
            u_s[rows, :] = jnp.where(hit, turned, u_s[rows, :])

    def put_cot(ref, slot, x, h):
        left, right = shifts(x, h)
        ref[slot, :DEEP, :] = right.astype(BF16)
        ref[slot, DEEP : 2 * DEEP, :] = x.astype(BF16)
        ref[slot, 2 * DEEP :, :] = left.astype(BF16)

    def fill(row, carry):
        put_field(row + 2, x_ref[row].astype(F32), hx_ref[row].astype(F32))
        put_cot(r_s, ROWS - row, r_ref[row].astype(F32), hr_ref[row].astype(F32))
        return carry

    lax.fori_loop(0, ROWS, fill, 0)
    blank = jnp.zeros((DEEP - SENT, LANES), F32)

    def unpack(first, second):
        cells = [
            jnp.concatenate(
                [jnp.where(low, first[k].astype(F32), second[k].astype(F32)), blank], axis=0
            )
            for k in range(4)
        ]
        sides = [pltpu.roll(cells[3], LANES - turn, 1) for turn in (4, 8)]
        return cells + sides

    up, down = unpack(pa_ref, pb_ref), unpack(pb_ref, pa_ref)
    put_field(1, up[0], up[3])
    put_field(0, up[1], up[4])
    put_field(ROWS + 2, down[0], down[3])
    put_field(ROWS + 3, down[1], down[4])
    put_cot(r_s, ROWS + 1, jnp.where(north, 0.0, up[2]), jnp.where(north, 0.0, up[5]))
    put_cot(r_s, 0, jnp.where(south, 0.0, down[2]), jnp.where(south, 0.0, down[5]))
    put_cot(pole_s, 0, jnp.where(north, up[2], 0.0), jnp.where(north, up[5], 0.0))
    put_cot(pole_s, 1, jnp.where(south, down[2], 0.0), jnp.where(south, down[5], 0.0))

    we, gt = we_ref[...], gt_ref[...]

    def band(slot):
        return f_s[slot].astype(F32)

    def swapped(flag, first, last):
        return jnp.where(flag, last, first).astype(BF16), jnp.where(flag, first, last).astype(BF16)

    def silu(v):
        return v * (1.0 / (1.0 + jnp.exp(-v)))

    n0, n2 = swapped(north, band(0), band(2))
    s0, s2 = swapped(south, band(ROWS + 1), band(ROWS + 3))
    ring = jnp.concatenate(
        [
            jnp.concatenate([n0, f_s[1], n2], axis=0),
            jnp.concatenate([s0, f_s[ROWS + 2], s2], axis=0),
        ],
        axis=1,
    )
    halo = silu(dot(we, ring)).astype(BF16)
    hid_ref[0] = halo[:, :LANES]
    hid_ref[ROWS + 1] = halo[:, LANES:]

    u = u_s[...]
    u2 = pltpu.roll(u, LANES - 2, 1)
    u4 = pltpu.roll(u, LANES - 4, 1)
    wide = lane_of(u.shape)
    last = 2 * (ROWS + 1)
    flip = (north & (wide < 2)) | (south & ((wide == last) | (wide == last + 1)))
    strip = jnp.concatenate(
        [jnp.where(flip, u4, u).astype(BF16), u2.astype(BF16), jnp.where(flip, u, u4).astype(BF16)],
        axis=0,
    )
    strip_ref[...] = silu(dot(we, strip)).astype(BF16)

    fx_s[:, :LANES] = dot(gt[:, :BAND], pole_s[0])
    fx_s[:, LANES:] = dot(gt[:, 2 * BAND :], pole_s[1])
    acc_s[...] = jnp.zeros_like(acc_s)

    def two(ref, first, second):
        a = ref[pl.ds(first, 3)].reshape(TAPS, LANES)
        b = ref[pl.ds(second, 3)].reshape(TAPS, LANES)
        return jnp.concatenate([a, b], axis=1)

    half = lane_of(fx_s.shape) < LANES

    def step(pair, carry):
        f2 = two(f_s, 2 * pair + 1, 2 * pair + 2)
        r2 = two(r_s, ROWS - 1 - 2 * pair, ROWS - 2 - 2 * pair)
        pre = dot(we_ref[...], f2)
        gate = 1.0 / (1.0 + jnp.exp(-pre))
        hid = (pre * gate).astype(BF16)
        edge = ((pair == 0) & half) | ((pair == ROWS // 2 - 1) & ~half)
        feat = (dot(gt_ref[...], r2) + jnp.where(edge, fx_s[...], 0.0)).astype(BF16)
        feat_ref[2 * pair] = feat[:, :LANES]
        feat_ref[2 * pair + 1] = feat[:, LANES:]
        hid_ref[2 * pair + 1] = hid[:, :LANES]
        hid_ref[2 * pair + 2] = hid[:, LANES:]
        back = (feat.astype(F32) * gate * (1.0 + pre * (1.0 - gate))).astype(BF16)
        acc_s[0] += dot(r2, hid, NT)
        acc_s[1] += dot(f2, back, NT)
        return carry

    lax.fori_loop(0, ROWS // 2, step, 0)
    acc_s[0, :BAND, :] += dot(pole_s[0], hid_ref[1], NT)
    acc_s[0, 2 * BAND :, :] += dot(pole_s[1], hid_ref[ROWS], NT)

    def pack(which, out_ref):
        for tap in range(9):
            pack_s[69 * tap : 69 * tap + 69, :] = acc_s[which, DEEP * tap : DEEP * tap + 69, :]
        pack_s[621:, :] = jnp.zeros((pack_s.shape[0] - 621, pack_s.shape[1]), F32)
        out_ref[:PACK, :] = pack_s[:PACK, :LANES].astype(out_ref.dtype)
        out_ref[PACK:, :] = pack_s[:PACK, LANES:].astype(out_ref.dtype)

    pack(1 - core, sent_ref)
    pack(core, kept_ref)


def rebuilt_kernel(hid_ref, strip_ref, ga_ref, out_ref, z_s, t_s, out_s):
    ga = ga_ref[...]
    zs = dot(ga, strip_ref[...])
    t0 = zs[:DEEP]
    t2 = zs[2 * DEEP : BAND]
    for a in (1, 2):
        t0 = t0 + pltpu.roll(zs[a * BAND : a * BAND + DEEP], LANES - 2 * a, 1)
        t2 = t2 + pltpu.roll(zs[a * BAND + 2 * DEEP : (a + 1) * BAND], LANES - 2 * a, 1)
    lane = lane_of((DEEP, LANES))
    even = lax.rem(lane, 2) == 0
    t_s[...] = jnp.where(even, pltpu.roll(t2, LANES - 1, 1), pltpu.roll(t0, 1, 1))

    def fill(pair, carry):
        z = dot(ga, jnp.concatenate([hid_ref[2 * pair], hid_ref[2 * pair + 1]], axis=1))
        z_s[2 * pair] = z[:, :LANES]
        z_s[2 * pair + 1] = z[:, LANES:]
        return carry

    lax.fori_loop(0, ROWS // 2 + 1, fill, 0)

    def emit(row, carry):
        sums = []
        for b in range(3):
            total = z_s[row, b * DEEP : (b + 1) * DEEP, :]
            for a in (1, 2):
                start = a * BAND + b * DEEP
                total = total + z_s[row + a, start : start + DEEP, :]
            sums.append(total)
        out = sums[1]
        out = out + jnp.where(lane == 0, 0.0, pltpu.roll(sums[0], 1, 1))
        out = out + jnp.where(lane == LANES - 1, 0.0, pltpu.roll(sums[2], LANES - 1, 1))
        side = pltpu.roll(t_s[...], LANES - 1 - 2 * row, 1)
        out = out + jnp.where((lane == 0) | (lane == LANES - 1), side, 0.0)
        out_s[pl.ds(row, DEEP, stride=ROWS), :] = out
        return carry

    lax.fori_loop(0, ROWS, emit, 0)
    size = out_ref.shape[0] * ROWS
    out_ref[...] = out_s[:size, :].reshape(out_ref.shape).astype(BF16)


def turn_kernel(rows_ref, out_ref, out_s):
    for row in range(ROWS):
        out_s[pl.ds(row, out_ref.shape[0], stride=ROWS), :] = rows_ref[row].astype(F32)
    out_ref[...] = out_s[...].reshape(out_ref.shape).astype(BF16)


def total_kernel(pieces_ref, out_ref):
    total = pieces_ref[0].astype(F32)
    for k in range(1, pieces_ref.shape[0]):
        total = total + pieces_ref[k].astype(F32)
    total = total.astype(BF16)
    for k in range(out_ref.shape[0]):
        out_ref[k] = total


def final_kernel(norm, flags_ref, own_ref, other_ref, enc_ref, gen_ref, pack_s):
    first = flags_ref[2] == 0
    own, other = own_ref[...].astype(F32), other_ref[...].astype(F32)
    gen = jnp.where(first, own, other) * norm
    enc = jnp.where(first, other, own) * norm
    for value, out in ((gen, gen_ref), (enc, enc_ref)):
        pack_s[...] = value
        for tap in range(9):
            out[tap, :, :LANES] = pack_s[69 * tap : 69 * tap + 69, :]
            out[tap, :, LANES:] = pack_s[PACK + 69 * tap : PACK + 69 * tap + 69, :]


def swap_cores(value):
    return lax.ppermute(value, "core", [(0, 1), (1, 0)])


def great_circles(lat_count, lon_count):
    pairs = []
    for la in range(lat_count):
        for lo in range(lon_count):
            if lo < lon_count // 2:
                to = (la + 1, lo) if la < lat_count - 1 else (la, lo + lon_count // 2)
            else:
                to = (la - 1, lo) if la > 0 else (la, lo - lon_count // 2)
            pairs.append((la * lon_count + lo, to[0] * lon_count + to[1]))
    return pairs, [(b, a) for a, b in pairs]


def on_device(fields, enc_kernel, gen_kernel, recon_grad):
    variables, height, width = fields.shape
    channels = gen_kernel.shape[3]
    lat_index, lat_count = lax.axis_index(LAT), lax.axis_size(LAT)
    lon_count = lax.axis_size(LON)
    core = lax.axis_index("core")
    low = lax.axis_index("y_lo") == 0
    flags = jnp.stack(
        [
            (lat_index == 0).astype(jnp.int32),
            (lat_index == lat_count - 1).astype(jnp.int32),
            core.astype(jnp.int32),
            low.astype(jnp.int32),
        ]
    )
    pad = ((0, 0), (0, 0), (0, DEEP - variables), (0, 0))
    gen_rows = jnp.pad(gen_kernel, pad).reshape(TAPS, channels)
    enc_rows = jnp.pad(jnp.swapaxes(enc_kernel, 2, 3), pad).reshape(TAPS, channels)
    plane = jax.ShapeDtypeStruct((ROWS, DEEP, LANES), BF16)
    side = jax.ShapeDtypeStruct((8, ROWS * DEEP), BF16)
    x, r, east, west = call(
        columns_kernel, (plane, plane, side, side), 10**7, [pltpu.VMEM((ROWS * DEEP, LANES), F32)]
    )(in_specs=[FULL] * 2, out_specs=(FULL,) * 4)(fields, recon_grad)
    right = [(i, (i + 1) % lon_count) for i in range(lon_count)]
    left = [(b, a) for a, b in right]
    from_left = lax.ppermute(east, LON, right)
    from_right = lax.ppermute(west, LON, left)
    packet = jax.ShapeDtypeStruct((4, SENT, LANES), BF16)
    hx, hr, pa, pb = call(rows_kernel, (plane, plane, packet, packet), 10**7)(
        in_specs=[FLAGS] + [FULL] * 4, out_specs=(FULL,) * 4
    )(flags, x, r, from_left, from_right)
    ahead, behind = great_circles(lat_count, lon_count)
    pa = lax.ppermute(pa, LAT + LON, ahead)
    pb = lax.ppermute(pb, LAT + LON, behind)

    packed = (2 * PACK, LANES)
    feat, hid, strip, sent, kept = call(
        main_kernel,
        (
            jax.ShapeDtypeStruct((ROWS, channels, LANES), BF16),
            jax.ShapeDtypeStruct((ROWS + 2, channels, LANES), BF16),
            jax.ShapeDtypeStruct((channels, LANES), BF16),
            jax.ShapeDtypeStruct(packed, BF16),
            jax.ShapeDtypeStruct(packed, F32),
        ),
        3 * 10**9,
        [
            pltpu.VMEM((ROWS + 4, BAND, LANES), BF16),
            pltpu.VMEM((ROWS + 2, BAND, LANES), BF16),
            pltpu.VMEM((2, BAND, LANES), BF16),
            pltpu.VMEM((BAND, LANES), F32),
            pltpu.VMEM((channels, 2 * LANES), F32),
            pltpu.VMEM((2, TAPS, channels), F32),
            pltpu.VMEM((PACK + 8, channels), F32),
        ],
        24,
    )(in_specs=[FLAGS] + [FULL] * 8, out_specs=(FULL,) * 5)(
        flags, x, r, hx, hr, pa, pb, enc_rows.T, gen_rows.T
    )
    rebuilt = call(
        rebuilt_kernel,
        jax.ShapeDtypeStruct((variables, height, width), BF16),
        4 * 10**9,
        [
            pltpu.VMEM((ROWS + 2, TAPS, LANES), F32),
            pltpu.VMEM((DEEP, LANES), F32),
            pltpu.VMEM((DEEP * ROWS, LANES), F32),
        ],
        12,
    )(in_specs=[FULL] * 3, out_specs=FULL)(hid, strip, gen_rows)
    feat_grad = call(
        turn_kernel,
        jax.ShapeDtypeStruct((channels, height, width), BF16),
        2 * 10**9,
        [pltpu.VMEM((channels * ROWS, LANES), F32)],
    )(in_specs=[FULL], out_specs=FULL)(feat)

    half = (kept + swap_cores(sent).astype(F32)).astype(BF16)
    faces, layers = lax.axis_size(FACE), lax.axis_size("z")
    piece = (2 * PACK // faces, LANES)

    def exchange(value, axes):
        return lax.all_to_all(value, axes, 0, 0, tiled=True)

    def total(pieces, copies):
        return call(total_kernel, jax.ShapeDtypeStruct((copies,) + piece, BF16), 10**7)(
            in_specs=[FULL], out_specs=FULL
        )(pieces)

    pieces = exchange(half.reshape((faces,) + piece), FACE)
    pieces, rebuilt = lax.optimization_barrier((pieces, rebuilt))
    pieces = exchange(total(pieces, layers), "z")
    pieces, feat_grad = lax.optimization_barrier((pieces, feat_grad))
    own = exchange(total(pieces, faces), FACE).reshape(packed)
    other = swap_cores(own)
    norm = (height * lat_count * width * lon_count) ** -0.5
    grad = jax.ShapeDtypeStruct((9, variables, channels), F32)
    enc, gen = call(
        functools.partial(final_kernel, norm), (grad, grad), 10**7, [pltpu.VMEM(packed, F32)]
    )(in_specs=[FLAGS, FULL, FULL], out_specs=(FULL, FULL))(flags, own, other)
    shape = (3, 3, variables, channels)
    return (rebuilt, feat_grad, jnp.swapaxes(enc.reshape(shape), 2, 3), gen.reshape(shape))


def solution(mesh):
    lat_count, lon_count = mesh.shape["lat"], mesh.shape["lon"]
    fine = Mesh(mesh.devices.reshape(lat_count // 2, 2, 2, lon_count // 4, 2), LAT + LON)
    return jax.shard_map(
        on_device,
        mesh=fine,
        in_specs=(P(None, LAT, LON), P(), P(), P(None, LAT, LON)),
        out_specs=(P(None, LAT, LON), P(None, LAT, LON), P(), P()),
        check_vma=False,
    )
```

```python
import functools

import jax
import jax.numpy as jnp
from jax import lax
from jax.experimental import pallas as pl
from jax.experimental.pallas import tpu as pltpu
from jax.sharding import Mesh
from jax.sharding import PartitionSpec as P

FACE = ("y_hi", "y_lo", "x")
LAT = ("z", "y_hi")
LON = ("y_lo", "x", "core")

LANES = 128
ROWS = 16
DEEP = 80
SENT = 72
SIDES = 16
MID = ROWS - 2
BAND = 3 * DEEP
TAPS = 3 * BAND
PACK = 640
F32 = jnp.float32
BF16 = jnp.bfloat16
NT = (((1,), (1,)), ((), ()))
TN = (((0,), (0,)), ((), ()))
FULL = pl.BlockSpec(memory_space=pltpu.VMEM)
FLAGS = pl.BlockSpec(memory_space=pltpu.SMEM)
FAR = pl.BlockSpec(memory_space=pltpu.HBM)


def lane_of(shape):
    return lax.broadcasted_iota(jnp.int32, shape, len(shape) - 1)


def dot(a, b, dims=(((1,), (0,)), ((), ()))):
    return lax.dot_general(a, b, dims, preferred_element_type=F32)


def call(kernel, outs, cost, scratch=(), limit=8):
    return functools.partial(
        pl.pallas_call,
        kernel,
        out_shape=outs,
        scratch_shapes=list(scratch),
        compiler_params=pltpu.CompilerParams(vmem_limit_bytes=limit << 20),
        cost_estimate=pl.CostEstimate(flops=cost, bytes_accessed=cost // 500, transcendentals=0),
    )


def picks(count, pairs):
    rows = lax.broadcasted_iota(jnp.int32, (SIDES, count), 0)
    lanes = lax.broadcasted_iota(jnp.int32, (SIDES, count), 1)
    hot = (rows == pairs[0][0]) & (lanes == pairs[0][1])
    for row, lane in pairs[1:]:
        hot = hot | ((rows == row) & (lanes == lane))
    return jnp.where(hot, 1.0, 0.0).astype(BF16)


def columns_kernel(
    fields_ref, cot_ref, x_ref, r_ref, east_ref, west_ref, in_x, in_r, raw_s, sems
):
    loads = [
        pltpu.make_async_copy(fields_ref, in_x, sems.at[0]),
        pltpu.make_async_copy(cot_ref, in_r, sems.at[1]),
    ]
    for load in loads:
        load.start()
    size = in_x.shape[0] * ROWS
    sides = None
    for load, source, target, chosen in (
        (loads[0], in_x, x_ref, [(0, 126), (1, 127), (8, 0), (9, 1)]),
        (loads[1], in_r, r_ref, [(2, 127), (10, 0)]),
    ):
        load.wait()
        raw_s[:size, :] = source[...].astype(F32).reshape(size, LANES)
        raw_s[size:, :] = jnp.zeros((raw_s.shape[0] - size, LANES), F32)
        for row in range(ROWS):
            target[row] = raw_s[pl.ds(row, DEEP, stride=ROWS), :].astype(BF16)
        some = dot(picks(LANES, chosen), target[...].reshape(ROWS * DEEP, LANES), NT)
        sides = some if sides is None else sides + some
    east_ref[...] = sides[: SIDES // 2].astype(BF16)
    west_ref[...] = sides[SIDES // 2 :].astype(BF16)


def side_columns(east_ref, west_ref, rows):
    first, last = rows[0] * DEEP, (rows[-1] + 1) * DEEP
    east, west = east_ref[:, first:last].astype(F32), west_ref[:, first:last].astype(F32)
    return jnp.concatenate([east, west], axis=0).T.astype(BF16)


OWN = [(0, 126), (1, 127), (8, 0), (9, 1)]


def side_planes(columns):
    return dot(columns, picks(2 * LANES, OWN + [(2, LANES + 127), (10, LANES)]))


def rows_kernel(flags_ref, x_ref, r_ref, east_ref, west_ref, a_ref, b_ref):
    low = flags_ref[3] == 1
    edge_picks = picks(LANES, OWN + [(2, 7), (10, 8)])
    inner_picks = picks(LANES, [(0, 2), (1, 3), (8, 4), (9, 5)])

    def packet(edge, inner):
        both = side_columns(east_ref, west_ref, sorted((edge, inner)))
        outer, other = (both[:DEEP], both[DEEP:]) if edge < inner else (both[DEEP:], both[:DEEP])
        sides = dot(outer, edge_picks) + dot(other, inner_picks)
        return [x_ref[edge].astype(F32), x_ref[inner].astype(F32), r_ref[edge].astype(F32), sides]

    top, bottom = packet(0, 1), packet(ROWS - 1, ROWS - 2)
    for k in range(4):
        t, b = top[k][:SENT], bottom[k][:SENT]
        a_ref[k] = jnp.where(low, b, t).astype(BF16)
        b_ref[k] = jnp.where(low, t, b).astype(BF16)


def shifts(x, h):
    lane = lane_of(x.shape)
    left = pltpu.roll(jnp.where(lane == LANES - 1, h, x), 1, 1)
    right = pltpu.roll(jnp.where(lane == 0, h, x), LANES - 1, 1)
    return left, right


def put_field(ref, slot, x, h):
    left, right = shifts(x, h)
    ref[slot, :DEEP, :] = left.astype(BF16)
    ref[slot, DEEP : 2 * DEEP, :] = x.astype(BF16)
    ref[slot, 2 * DEEP :, :] = right.astype(BF16)


def put_cot(ref, slot, x, h):
    left, right = shifts(x, h)
    ref[slot, :DEEP, :] = right.astype(BF16)
    ref[slot, DEEP : 2 * DEEP, :] = x.astype(BF16)
    ref[slot, 2 * DEEP :, :] = left.astype(BF16)


def put_strip(ref, slot, x, h):
    lane = lane_of((DEEP, LANES))
    spot = 2 * slot
    hit = (lane == spot) | (lane == spot + 1)
    sides = (
        (jnp.where(lane == LANES - 1, x, h), spot + 2),
        (h, spot + 1),
        (jnp.where(lane == 0, x, h), spot),
    )
    for tap, (plane, turn) in enumerate(sides):
        rows = pl.ds(tap * DEEP, DEEP)
        ref[rows, :] = jnp.where(hit, pltpu.roll(plane, turn, 1), ref[rows, :])


def wide(ref, slots):
    return jnp.concatenate([ref[slot] for slot in slots], axis=1)


def stacks(ref, starts):
    return jnp.concatenate([ref[k : k + 3].reshape(TAPS, LANES) for k in starts], axis=1)


def inner_kernel(
    x_ref, r_ref, east_ref, west_ref, we_ref, gt_ref, feat_ref, hid_ref, acc_ref, f_s, r_s, back_s
):
    planes = side_planes(side_columns(east_ref, west_ref, range(ROWS)))
    for row in range(ROWS):
        side = planes[row * DEEP : (row + 1) * DEEP]
        put_field(f_s, row, x_ref[row].astype(F32), side[:, :LANES])
        put_cot(r_s, ROWS - 1 - row, r_ref[row].astype(F32), side[:, LANES:])
    for k in range(0, MID, 2):
        pre = dot(we_ref[...], stacks(f_s, (k, k + 1)))
        gate = 1.0 / (1.0 + jnp.exp(-pre))
        hid = (pre * gate).astype(BF16)
        feat = dot(gt_ref[...], stacks(r_s, (MID - 1 - k, MID - 2 - k))).astype(BF16)
        back = (feat.astype(F32) * gate * (1.0 + pre * (1.0 - gate))).astype(BF16)
        for ref, value in ((feat_ref, feat), (hid_ref, hid), (back_s, back)):
            ref[k] = value[:, :LANES]
            ref[k + 1] = value[:, LANES:]
    rows = range(MID)
    acc_ref[0] = dot(stacks(r_s, [MID - 1 - k for k in rows]), wide(hid_ref, rows), NT)
    acc_ref[1] = dot(stacks(f_s, rows), wide(back_s, rows), NT)


def unpack(low, first_ref, second_ref):
    blank = jnp.zeros((DEEP - SENT, LANES), F32)
    cells = [
        jnp.concatenate(
            [jnp.where(low, first_ref[k].astype(F32), second_ref[k].astype(F32)), blank], axis=0
        )
        for k in range(4)
    ]
    return cells + [pltpu.roll(cells[3], LANES - turn, 1) for turn in (4, 8)]


def edge_kernel(
    flags_ref, x_ref, r_ref, east_ref, west_ref, pa_ref, pb_ref, we_ref, gt_ref, acc_ref,
    feat_ref, hid_ref, sent_ref, kept_ref, f_s, r_s, pole_s, sum_s, pack_s,
):
    north, south = flags_ref[0] == 1, flags_ref[1] == 1
    core, low = flags_ref[2], flags_ref[3] == 1
    up, down = unpack(low, pa_ref, pb_ref), unpack(low, pb_ref, pa_ref)
    near = [side_planes(side_columns(east_ref, west_ref, rows)) for rows in ((0, 1), (14, 15))]
    slots = {0: (0, 0), 1: (0, DEEP), ROWS - 2: (1, 0), ROWS - 1: (1, DEEP)}
    for row, slot, back in ((0, 1, 1), (1, 2, 0), (ROWS - 2, 3, 5), (ROWS - 1, 4, 4)):
        which, start = slots[row]
        planes = near[which][start : start + DEEP]
        put_field(f_s, slot, x_ref[row].astype(F32), planes[:, :LANES])
        put_cot(r_s, back, r_ref[row].astype(F32), planes[:, LANES:])
    put_field(f_s, 0, up[0], up[3])
    put_field(f_s, 5, down[0], down[3])
    put_cot(r_s, 2, jnp.where(north, 0.0, up[2]), jnp.where(north, 0.0, up[5]))
    put_cot(r_s, 3, jnp.where(south, 0.0, down[2]), jnp.where(south, 0.0, down[5]))
    put_cot(pole_s, 0, jnp.where(north, up[2], 0.0), jnp.where(north, up[5], 0.0))
    put_cot(pole_s, 1, jnp.where(south, down[2], 0.0), jnp.where(south, down[5], 0.0))
    f2, r2 = stacks(f_s, (0, 3)), stacks(r_s, (0, 3))
    pre = dot(we_ref[...], f2)
    gate = 1.0 / (1.0 + jnp.exp(-pre))
    hid = (pre * gate).astype(BF16)
    hid_ref[0], hid_ref[1] = hid[:, :LANES], hid[:, LANES:]
    extra = jnp.concatenate(
        [dot(gt_ref[:, :BAND], pole_s[0]), dot(gt_ref[:, 2 * BAND :], pole_s[1])], axis=1
    )
    feat = (dot(gt_ref[...], r2) + extra).astype(BF16)
    feat_ref[0], feat_ref[1] = feat[:, :LANES], feat[:, LANES:]
    back = (feat.astype(F32) * gate * (1.0 + pre * (1.0 - gate))).astype(BF16)
    sum_s[0] = acc_ref[0] + dot(r2, hid, NT)
    sum_s[1] = acc_ref[1] + dot(f2, back, NT)
    sum_s[0, :BAND, :] += dot(pole_s[0], hid_ref[0], NT)
    sum_s[0, 2 * BAND :, :] += dot(pole_s[1], hid_ref[1], NT)

    def pack(which, out_ref):
        for tap in range(9):
            pack_s[69 * tap : 69 * tap + 69, :] = sum_s[which, DEEP * tap : DEEP * tap + 69, :]
        pack_s[621:, :] = jnp.zeros((pack_s.shape[0] - 621, pack_s.shape[1]), F32)
        out_ref[:PACK, :] = pack_s[:PACK, :LANES].astype(out_ref.dtype)
        out_ref[PACK:, :] = pack_s[:PACK, LANES:].astype(out_ref.dtype)

    pack(1 - core, sent_ref)
    pack(core, kept_ref)


def beyond_kernel(
    flags_ref, x_ref, east_ref, west_ref, pa_ref, pb_ref, we_ref, halo_ref, strip_ref, f_s, u_s
):
    north, south, low = flags_ref[0] == 1, flags_ref[1] == 1, flags_ref[3] == 1
    up, down = unpack(low, pa_ref, pb_ref), unpack(low, pb_ref, pa_ref)
    planes = side_planes(side_columns(east_ref, west_ref, range(ROWS)))
    u_s[...] = jnp.zeros_like(u_s)
    kept = {0: 2, 1: 3, ROWS - 2: 4, ROWS - 1: 5}
    for row in range(ROWS):
        x, h = x_ref[row].astype(F32), planes[row * DEEP : (row + 1) * DEEP, :LANES]
        put_strip(u_s, row + 2, x, h)
        if row in kept:
            put_field(f_s, kept[row], x, h)
    for slot, place, x, h in (
        (0, 0, up[1], up[4]),
        (1, 1, up[0], up[3]),
        (6, ROWS + 2, down[0], down[3]),
        (7, ROWS + 3, down[1], down[4]),
    ):
        put_field(f_s, slot, x, h)
        put_strip(u_s, place, x, h)

    def rows(flag, first, middle, last):
        a, c = f_s[first].astype(F32), f_s[last].astype(F32)
        ends = jnp.where(flag, c, a).astype(BF16), jnp.where(flag, a, c).astype(BF16)
        return jnp.concatenate([ends[0], f_s[middle], ends[1]], axis=0)

    def silu(v):
        return (v * (1.0 / (1.0 + jnp.exp(-v)))).astype(BF16)

    ring = jnp.concatenate([rows(north, 0, 1, 2), rows(south, 5, 6, 7)], axis=1)
    halo = silu(dot(we_ref[...], ring))
    halo_ref[0], halo_ref[1] = halo[:, :LANES], halo[:, LANES:]
    u = u_s[...]
    u2 = pltpu.roll(u, LANES - 2, 1)
    u4 = pltpu.roll(u, LANES - 4, 1)
    lane = lane_of(u.shape)
    last = 2 * (ROWS + 1)
    flip = (north & (lane < 2)) | (south & ((lane == last) | (lane == last + 1)))
    strip = jnp.concatenate(
        [jnp.where(flip, u4, u).astype(BF16), u2.astype(BF16), jnp.where(flip, u, u4).astype(BF16)],
        axis=0,
    )
    strip_ref[...] = silu(dot(we_ref[...], strip))


def rebuilt_kernel(mid_ref, edge_ref, halo_ref, strip_ref, ga_ref, out_ref, z_s, t_s, out_s):
    ga = ga_ref[...]
    zs = dot(ga, strip_ref[...])
    t0 = zs[:DEEP]
    t2 = zs[2 * DEEP : BAND]
    for a in (1, 2):
        t0 = t0 + pltpu.roll(zs[a * BAND : a * BAND + DEEP], LANES - 2 * a, 1)
        t2 = t2 + pltpu.roll(zs[a * BAND + 2 * DEEP : (a + 1) * BAND], LANES - 2 * a, 1)
    lane = lane_of((DEEP, LANES))
    even = lax.rem(lane, 2) == 0
    t_s[...] = jnp.where(even, pltpu.roll(t2, LANES - 1, 1), pltpu.roll(t0, 1, 1))

    def put(slot, first, second):
        z = dot(ga_ref[...], jnp.concatenate([first, second], axis=1))
        z_s[slot] = z[:, :LANES]
        z_s[slot + 1] = z[:, LANES:]

    put(0, halo_ref[0], edge_ref[0])
    for k in range(0, MID, 2):
        put(k + 2, mid_ref[k], mid_ref[k + 1])
    put(ROWS, edge_ref[1], halo_ref[1])

    for row in range(ROWS):
        sums = []
        for b in range(3):
            total = z_s[row, b * DEEP : (b + 1) * DEEP, :]
            for a in (1, 2):
                start = a * BAND + b * DEEP
                total = total + z_s[row + a, start : start + DEEP, :]
            sums.append(total)
        out = sums[1]
        out = out + jnp.where(lane == 0, 0.0, pltpu.roll(sums[0], 1, 1))
        out = out + jnp.where(lane == LANES - 1, 0.0, pltpu.roll(sums[2], LANES - 1, 1))
        side = pltpu.roll(t_s[...], LANES - 1 - 2 * row, 1)
        out = out + jnp.where((lane == 0) | (lane == LANES - 1), side, 0.0)
        out_s[pl.ds(row, DEEP, stride=ROWS), :] = out
    size = out_ref.shape[0] * ROWS
    out_ref[...] = out_s[:size, :].reshape(out_ref.shape).astype(BF16)


def turn_kernel(mid_ref, edge_ref, out_ref, out_s):
    rows = [edge_ref.at[0]] + [mid_ref.at[row] for row in range(MID)] + [edge_ref.at[1]]
    for row in range(ROWS):
        out_s[pl.ds(row, out_ref.shape[0], stride=ROWS), :] = rows[row][...].astype(F32)
    out_ref[...] = out_s[...].reshape(out_ref.shape).astype(BF16)


def total_kernel(pieces_ref, out_ref):
    total = pieces_ref[0].astype(F32)
    for k in range(1, pieces_ref.shape[0]):
        total = total + pieces_ref[k].astype(F32)
    total = total.astype(BF16)
    for k in range(out_ref.shape[0]):
        out_ref[k] = total


def final_kernel(norm, flags_ref, own_ref, other_ref, enc_ref, gen_ref, pack_s):
    first = flags_ref[2] == 0
    own, other = own_ref[...].astype(F32), other_ref[...].astype(F32)
    gen = jnp.where(first, own, other) * norm
    enc = jnp.where(first, other, own) * norm
    for value, out in ((gen, gen_ref), (enc, enc_ref)):
        pack_s[...] = value
        for tap in range(9):
            out[tap, :, :LANES] = pack_s[69 * tap : 69 * tap + 69, :]
            out[tap, :, LANES:] = pack_s[PACK + 69 * tap : PACK + 69 * tap + 69, :]


def swap_cores(value):
    return lax.ppermute(value, "core", [(0, 1), (1, 0)])


def great_circles(lat_count, lon_count):
    pairs = []
    for la in range(lat_count):
        for lo in range(lon_count):
            if lo < lon_count // 2:
                to = (la + 1, lo) if la < lat_count - 1 else (la, lo + lon_count // 2)
            else:
                to = (la - 1, lo) if la > 0 else (la, lo - lon_count // 2)
            pairs.append((la * lon_count + lo, to[0] * lon_count + to[1]))
    return pairs, [(b, a) for a, b in pairs]


def on_device(fields, enc_kernel, gen_kernel, recon_grad):
    variables, height, width = fields.shape
    channels = gen_kernel.shape[3]
    lat_index, lat_count = lax.axis_index(LAT), lax.axis_size(LAT)
    lon_count = lax.axis_size(LON)
    core = lax.axis_index("core")
    low = lax.axis_index("y_lo") == 0
    flags = jnp.stack(
        [
            (lat_index == 0).astype(jnp.int32),
            (lat_index == lat_count - 1).astype(jnp.int32),
            core.astype(jnp.int32),
            low.astype(jnp.int32),
        ]
    )
    pad = ((0, 0), (0, 0), (0, DEEP - variables), (0, 0))
    gen_rows = jnp.pad(gen_kernel, pad).reshape(TAPS, channels)
    enc_rows = jnp.pad(jnp.swapaxes(enc_kernel, 2, 3), pad).reshape(TAPS, channels)
    def shaped(*shape, dtype=BF16):
        return jax.ShapeDtypeStruct(shape, dtype)

    plane, side = shaped(ROWS, DEEP, LANES), shaped(SIDES // 2, ROWS * DEEP)
    x, r, east, west = call(
        columns_kernel,
        (plane, plane, side, side),
        10**7,
        [
            pltpu.VMEM(fields.shape, BF16),
            pltpu.VMEM(fields.shape, BF16),
            pltpu.VMEM((ROWS * DEEP, LANES), F32),
            pltpu.SemaphoreType.DMA((2,)),
        ],
    )(in_specs=[FAR] * 2, out_specs=(FULL,) * 4)(
        *(pltpu.with_memory_space_constraint(v, pltpu.HBM) for v in (fields, recon_grad))
    )
    right = [(i, (i + 1) % lon_count) for i in range(lon_count)]
    left = [(b, a) for a, b in right]
    east = lax.ppermute(east, LON, right)
    west = lax.ppermute(west, LON, left)
    packet = shaped(4, SENT, LANES)
    pa, pb = call(rows_kernel, (packet, packet), 10**7)(
        in_specs=[FLAGS] + [FULL] * 4, out_specs=(FULL,) * 2
    )(flags, x, r, east, west)
    ahead, behind = great_circles(lat_count, lon_count)
    pa = lax.ppermute(pa, LAT + LON, ahead)
    pb = lax.ppermute(pb, LAT + LON, behind)
    we, gt = enc_rows.T, gen_rows.T
    sums, packed = (2, TAPS, channels), (2 * PACK, LANES)
    feat_mid, hid_mid, acc = call(
        inner_kernel,
        (shaped(MID, channels, LANES), shaped(MID, channels, LANES), shaped(*sums, dtype=F32)),
        9 * 10**9,
        [
            pltpu.VMEM((ROWS, BAND, LANES), BF16),
            pltpu.VMEM((ROWS, BAND, LANES), BF16),
            pltpu.VMEM((MID, channels, LANES), BF16),
        ],
        16,
    )(in_specs=[FULL] * 6, out_specs=(FULL,) * 3)(x, r, east, west, we, gt)
    feat_edge, hid_edge, sent, kept = call(
        edge_kernel,
        (
            shaped(2, channels, LANES),
            shaped(2, channels, LANES),
            shaped(*packed),
            shaped(*packed, dtype=F32),
        ),
        10**9,
        [
            pltpu.VMEM((6, BAND, LANES), BF16),
            pltpu.VMEM((6, BAND, LANES), BF16),
            pltpu.VMEM((2, BAND, LANES), BF16),
            pltpu.VMEM(sums, F32),
            pltpu.VMEM((PACK + 8, channels), F32),
        ],
        16,
    )(in_specs=[FLAGS] + [FULL] * 9, out_specs=(FULL,) * 4)(
        flags, x, r, east, west, pa, pb, we, gt, acc
    )
    halo, strip = call(
        beyond_kernel,
        (shaped(2, channels, LANES), shaped(channels, LANES)),
        10**9,
        [pltpu.VMEM((8, BAND, LANES), BF16), pltpu.VMEM((BAND, LANES), F32)],
    )(in_specs=[FLAGS] + [FULL] * 6, out_specs=(FULL,) * 2)(flags, x, east, west, pa, pb, we)
    feat_grad = call(
        turn_kernel,
        shaped(channels, height, width),
        2 * 10**9,
        [pltpu.VMEM((channels * ROWS, LANES), F32)],
    )(in_specs=[FULL] * 2, out_specs=FULL)(feat_mid, feat_edge)

    half = (kept + swap_cores(sent).astype(F32)).astype(BF16)
    faces, layers = lax.axis_size(FACE), lax.axis_size("z")
    piece = (2 * PACK // faces, LANES)

    def exchange(value, axes):
        return lax.all_to_all(value, axes, 0, 0, tiled=True)

    def total(pieces, copies):
        return call(total_kernel, jax.ShapeDtypeStruct((copies,) + piece, BF16), 10**7)(
            in_specs=[FULL], out_specs=FULL
        )(pieces)

    pieces = exchange(half.reshape((faces,) + piece), FACE)
    pieces, feat_grad, halo, strip = lax.optimization_barrier((pieces, feat_grad, halo, strip))
    pieces = exchange(total(pieces, layers), "z")
    rebuilt = call(
        rebuilt_kernel,
        shaped(variables, height, width),
        4 * 10**9,
        [
            pltpu.VMEM((ROWS + 2, TAPS, LANES), F32),
            pltpu.VMEM((DEEP, LANES), F32),
            pltpu.VMEM((DEEP * ROWS, LANES), F32),
        ],
        12,
    )(in_specs=[FULL] * 5, out_specs=FULL)(hid_mid, hid_edge, halo, strip, gen_rows)
    pieces, rebuilt = lax.optimization_barrier((pieces, rebuilt))
    own = exchange(total(pieces, faces), FACE).reshape(packed)
    other = swap_cores(own)
    norm = (height * lat_count * width * lon_count) ** -0.5
    grad = jax.ShapeDtypeStruct((9, variables, channels), F32)
    enc, gen = call(
        functools.partial(final_kernel, norm), (grad, grad), 10**7, [pltpu.VMEM(packed, F32)]
    )(in_specs=[FLAGS, FULL, FULL], out_specs=(FULL, FULL))(flags, own, other)
    shape = (3, 3, variables, channels)
    return (rebuilt, feat_grad, jnp.swapaxes(enc.reshape(shape), 2, 3), gen.reshape(shape))


def solution(mesh):
    lat_count, lon_count = mesh.shape["lat"], mesh.shape["lon"]
    fine = Mesh(mesh.devices.reshape(lat_count // 2, 2, 2, lon_count // 4, 2), LAT + LON)
    return jax.shard_map(
        on_device,
        mesh=fine,
        in_specs=(P(None, LAT, LON), P(), P(), P(None, LAT, LON)),
        out_specs=(P(None, LAT, LON), P(None, LAT, LON), P(), P()),
        check_vma=False,
    )
```

```python
import functools

import jax
import jax.numpy as jnp
from jax import lax
from jax.experimental import pallas as pl
from jax.experimental.pallas import tpu as pltpu
from jax.sharding import Mesh
from jax.sharding import PartitionSpec as P

FACE = ("y_hi", "y_lo", "x")
LAT = ("z", "y_hi")
LON = ("y_lo", "x", "core")

LANES = 128
ROWS = 16
DEEP = 80
SENT = 72
SIDES = 16
MID = ROWS - 2
EDGES = (0, 1, ROWS - 2, ROWS - 1)
BAND = 3 * DEEP
TAPS = 3 * BAND
PACK = 640
F32 = jnp.float32
BF16 = jnp.bfloat16
NT = (((1,), (1,)), ((), ()))
TN = (((0,), (0,)), ((), ()))
FULL = pl.BlockSpec(memory_space=pltpu.VMEM)
FLAGS = pl.BlockSpec(memory_space=pltpu.SMEM)
FAR = pl.BlockSpec(memory_space=pltpu.HBM)


def lane_of(shape):
    return lax.broadcasted_iota(jnp.int32, shape, len(shape) - 1)


def dot(a, b, dims=(((1,), (0,)), ((), ()))):
    return lax.dot_general(a, b, dims, preferred_element_type=F32)


def call(kernel, outs, cost, scratch=(), limit=8):
    return functools.partial(
        pl.pallas_call,
        kernel,
        out_shape=outs,
        scratch_shapes=list(scratch),
        compiler_params=pltpu.CompilerParams(vmem_limit_bytes=limit << 20),
        cost_estimate=pl.CostEstimate(flops=cost, bytes_accessed=cost // 500, transcendentals=0),
    )


def picks(count, pairs):
    rows = lax.broadcasted_iota(jnp.int32, (SIDES, count), 0)
    lanes = lax.broadcasted_iota(jnp.int32, (SIDES, count), 1)
    hot = (rows == pairs[0][0]) & (lanes == pairs[0][1])
    for row, lane in pairs[1:]:
        hot = hot | ((rows == row) & (lanes == lane))
    return jnp.where(hot, 1.0, 0.0).astype(BF16)


def columns_kernel(
    fields_ref, cot_ref, x_ref, r_ref, east_ref, west_ref, in_x, in_r, raw_s, sems
):
    loads = [
        pltpu.make_async_copy(fields_ref, in_x, sems.at[0]),
        pltpu.make_async_copy(cot_ref, in_r, sems.at[1]),
    ]
    for load in loads:
        load.start()
    size = in_x.shape[0] * ROWS
    sides = None
    for load, source, target, chosen in (
        (loads[0], in_x, x_ref, [(0, 126), (1, 127), (8, 0), (9, 1)]),
        (loads[1], in_r, r_ref, [(2, 127), (10, 0)]),
    ):
        load.wait()
        raw_s[:size, :] = source[...].astype(F32).reshape(size, LANES)
        raw_s[size:, :] = jnp.zeros((raw_s.shape[0] - size, LANES), F32)
        for row in range(ROWS):
            target[row] = raw_s[pl.ds(row, DEEP, stride=ROWS), :].astype(BF16)
        some = dot(picks(LANES, chosen), target[...].reshape(ROWS * DEEP, LANES), NT)
        sides = some if sides is None else sides + some
    east_ref[...] = sides[: SIDES // 2].astype(BF16)
    west_ref[...] = sides[SIDES // 2 :].astype(BF16)


def side_columns(east_ref, west_ref, rows):
    first, last = rows[0] * DEEP, (rows[-1] + 1) * DEEP
    east, west = east_ref[:, first:last].astype(F32), west_ref[:, first:last].astype(F32)
    return jnp.concatenate([east, west], axis=0).T.astype(BF16)


OWN = [(0, 126), (1, 127), (8, 0), (9, 1)]


def side_planes(columns):
    return dot(columns, picks(2 * LANES, OWN + [(2, LANES + 127), (10, LANES)]))


def rows_kernel(flags_ref, x_ref, r_ref, east_ref, west_ref, a_ref, b_ref):
    low = flags_ref[3] == 1
    edge_picks = picks(LANES, OWN + [(2, 7), (10, 8)])
    inner_picks = picks(LANES, [(0, 2), (1, 3), (8, 4), (9, 5)])

    def packet(edge, inner):
        both = side_columns(east_ref, west_ref, sorted((edge, inner)))
        outer, other = (both[:DEEP], both[DEEP:]) if edge < inner else (both[DEEP:], both[:DEEP])
        sides = dot(outer, edge_picks) + dot(other, inner_picks)
        return [x_ref[edge].astype(F32), x_ref[inner].astype(F32), r_ref[edge].astype(F32), sides]

    top, bottom = packet(0, 1), packet(ROWS - 1, ROWS - 2)
    for k in range(4):
        t, b = top[k][:SENT], bottom[k][:SENT]
        a_ref[k] = jnp.where(low, b, t).astype(BF16)
        b_ref[k] = jnp.where(low, t, b).astype(BF16)


def shifts(x, h):
    lane = lane_of(x.shape)
    left = pltpu.roll(jnp.where(lane == LANES - 1, h, x), 1, 1)
    right = pltpu.roll(jnp.where(lane == 0, h, x), LANES - 1, 1)
    return left, right


def put_field(ref, slot, x, h):
    left, right = shifts(x, h)
    ref[slot, :DEEP, :] = left.astype(BF16)
    ref[slot, DEEP : 2 * DEEP, :] = x.astype(BF16)
    ref[slot, 2 * DEEP :, :] = right.astype(BF16)


def put_cot(ref, slot, x, h):
    left, right = shifts(x, h)
    ref[slot, :DEEP, :] = right.astype(BF16)
    ref[slot, DEEP : 2 * DEEP, :] = x.astype(BF16)
    ref[slot, 2 * DEEP :, :] = left.astype(BF16)


def put_strip(ref, slot, x, h):
    lane = lane_of((DEEP, LANES))
    spot = 2 * slot
    hit = (lane == spot) | (lane == spot + 1)
    sides = (
        (jnp.where(lane == LANES - 1, x, h), spot + 2),
        (h, spot + 1),
        (jnp.where(lane == 0, x, h), spot),
    )
    for tap, (plane, turn) in enumerate(sides):
        rows = pl.ds(tap * DEEP, DEEP)
        ref[rows, :] = jnp.where(hit, pltpu.roll(plane, turn, 1), ref[rows, :])


def wide(ref, slots):
    return jnp.concatenate([ref[slot] for slot in slots], axis=1)


def stacks(ref, starts):
    return jnp.concatenate([ref[k : k + 3].reshape(TAPS, LANES) for k in starts], axis=1)


def inner_kernel(
    x_ref, r_ref, east_ref, west_ref, we_ref, gt_ref,
    feat_ref, hid_ref, acc_ref, fe_ref, re_ref, f_s, r_s, back_s,
):
    planes = side_planes(side_columns(east_ref, west_ref, range(ROWS)))
    for row in range(ROWS):
        side = planes[row * DEEP : (row + 1) * DEEP]
        put_field(f_s, row, x_ref[row].astype(F32), side[:, :LANES])
        put_cot(r_s, ROWS - 1 - row, r_ref[row].astype(F32), side[:, LANES:])
    for k, row in enumerate(EDGES):
        fe_ref[k] = f_s[row]
        re_ref[k] = r_s[ROWS - 1 - row]
    for k in range(0, MID, 2):
        pre = dot(we_ref[...], stacks(f_s, (k, k + 1)))
        gate = 1.0 / (1.0 + jnp.exp(-pre))
        hid = (pre * gate).astype(BF16)
        feat = dot(gt_ref[...], stacks(r_s, (MID - 1 - k, MID - 2 - k))).astype(BF16)
        back = (feat.astype(F32) * gate * (1.0 + pre * (1.0 - gate))).astype(BF16)
        for ref, value in ((feat_ref, feat), (hid_ref, hid), (back_s, back)):
            ref[k] = value[:, :LANES]
            ref[k + 1] = value[:, LANES:]
    rows = range(MID)
    acc_ref[0] = dot(stacks(r_s, [MID - 1 - k for k in rows]), wide(hid_ref, rows), NT)
    acc_ref[1] = dot(stacks(f_s, rows), wide(back_s, rows), NT)


def unpack(low, first_ref, second_ref):
    blank = jnp.zeros((DEEP - SENT, LANES), F32)
    cells = [
        jnp.concatenate(
            [jnp.where(low, first_ref[k].astype(F32), second_ref[k].astype(F32)), blank], axis=0
        )
        for k in range(4)
    ]
    return cells + [pltpu.roll(cells[3], LANES - turn, 1) for turn in (4, 8)]


def gradient(which, acc_ref, lhs_ref, rhs_ref, pole_ref, sum_s, pack_s, out_ref):
    sum_s[...] = acc_ref[which] + dot(lhs_ref[which], rhs_ref[which], NT)
    for k, start in ((0, 0), (1, 2 * BAND)):
        pole = jnp.where(which == 0, pole_ref[k].astype(F32), 0.0).astype(BF16)
        hid = rhs_ref[0, :, k * LANES : (k + 1) * LANES]
        sum_s[start : start + BAND, :] += dot(pole, hid, NT)
    for tap in range(9):
        pack_s[69 * tap : 69 * tap + 69, :] = sum_s[DEEP * tap : DEEP * tap + 69, :]
    pack_s[621:, :] = jnp.zeros((pack_s.shape[0] - 621, pack_s.shape[1]), F32)
    out_ref[:PACK, :] = pack_s[:PACK, :LANES].astype(out_ref.dtype)
    out_ref[PACK:, :] = pack_s[:PACK, LANES:].astype(out_ref.dtype)


def edge_kernel(
    flags_ref, fe_ref, re_ref, pa_ref, pb_ref, we_ref, gt_ref, acc_ref,
    feat_ref, hid_ref, sent_ref, lhs_ref, rhs_ref, pole_ref, out_s, cot_s, sum_s, pack_s,
):
    north, south = flags_ref[0] == 1, flags_ref[1] == 1
    core, low = flags_ref[2], flags_ref[3] == 1
    up, down = unpack(low, pa_ref, pb_ref), unpack(low, pb_ref, pa_ref)
    put_field(out_s, 0, up[0], up[3])
    put_field(out_s, 1, down[0], down[3])
    put_cot(cot_s, 0, jnp.where(north, 0.0, up[2]), jnp.where(north, 0.0, up[5]))
    put_cot(cot_s, 1, jnp.where(south, 0.0, down[2]), jnp.where(south, 0.0, down[5]))
    put_cot(pole_ref, 0, jnp.where(north, up[2], 0.0), jnp.where(north, up[5], 0.0))
    put_cot(pole_ref, 1, jnp.where(south, down[2], 0.0), jnp.where(south, down[5], 0.0))

    def beside(first, second):
        return jnp.concatenate(
            [jnp.concatenate(first, axis=0), jnp.concatenate(second, axis=0)], axis=1
        )

    lhs_ref[0] = beside(
        (re_ref[1], re_ref[0], cot_s[0]), (cot_s[1], re_ref[3], re_ref[2])
    )
    lhs_ref[1] = beside((out_s[0], fe_ref[0], fe_ref[1]), (fe_ref[2], fe_ref[3], out_s[1]))
    pre = dot(we_ref[...], lhs_ref[1])
    gate = 1.0 / (1.0 + jnp.exp(-pre))
    hid = (pre * gate).astype(BF16)
    extra = jnp.concatenate(
        [dot(gt_ref[:, :BAND], pole_ref[0]), dot(gt_ref[:, 2 * BAND :], pole_ref[1])], axis=1
    )
    feat = (dot(gt_ref[...], lhs_ref[0]) + extra).astype(BF16)
    back = (feat.astype(F32) * gate * (1.0 + pre * (1.0 - gate))).astype(BF16)
    hid_ref[0], hid_ref[1] = hid[:, :LANES], hid[:, LANES:]
    feat_ref[0], feat_ref[1] = feat[:, :LANES], feat[:, LANES:]
    rhs_ref[0], rhs_ref[1] = hid, back
    gradient(1 - core, acc_ref, lhs_ref, rhs_ref, pole_ref, sum_s, pack_s, sent_ref)


def kept_kernel(flags_ref, acc_ref, lhs_ref, rhs_ref, pole_ref, kept_ref, sum_s, pack_s):
    gradient(flags_ref[2], acc_ref, lhs_ref, rhs_ref, pole_ref, sum_s, pack_s, kept_ref)


def beyond_kernel(
    flags_ref, x_ref, east_ref, west_ref, pa_ref, pb_ref, we_ref, halo_ref, strip_ref, f_s, u_s
):
    north, south, low = flags_ref[0] == 1, flags_ref[1] == 1, flags_ref[3] == 1
    up, down = unpack(low, pa_ref, pb_ref), unpack(low, pb_ref, pa_ref)
    planes = side_planes(side_columns(east_ref, west_ref, range(ROWS)))
    u_s[...] = jnp.zeros_like(u_s)
    kept = {0: 2, 1: 3, ROWS - 2: 4, ROWS - 1: 5}
    for row in range(ROWS):
        x, h = x_ref[row].astype(F32), planes[row * DEEP : (row + 1) * DEEP, :LANES]
        put_strip(u_s, row + 2, x, h)
        if row in kept:
            put_field(f_s, kept[row], x, h)
    for slot, place, x, h in (
        (0, 0, up[1], up[4]),
        (1, 1, up[0], up[3]),
        (6, ROWS + 2, down[0], down[3]),
        (7, ROWS + 3, down[1], down[4]),
    ):
        put_field(f_s, slot, x, h)
        put_strip(u_s, place, x, h)

    def rows(flag, first, middle, last):
        a, c = f_s[first].astype(F32), f_s[last].astype(F32)
        ends = jnp.where(flag, c, a).astype(BF16), jnp.where(flag, a, c).astype(BF16)
        return jnp.concatenate([ends[0], f_s[middle], ends[1]], axis=0)

    def silu(v):
        return (v * (1.0 / (1.0 + jnp.exp(-v)))).astype(BF16)

    ring = jnp.concatenate([rows(north, 0, 1, 2), rows(south, 5, 6, 7)], axis=1)
    halo = silu(dot(we_ref[...], ring))
    halo_ref[0], halo_ref[1] = halo[:, :LANES], halo[:, LANES:]
    u = u_s[...]
    u2 = pltpu.roll(u, LANES - 2, 1)
    u4 = pltpu.roll(u, LANES - 4, 1)
    lane = lane_of(u.shape)
    last = 2 * (ROWS + 1)
    flip = (north & (lane < 2)) | (south & ((lane == last) | (lane == last + 1)))
    strip = jnp.concatenate(
        [jnp.where(flip, u4, u).astype(BF16), u2.astype(BF16), jnp.where(flip, u, u4).astype(BF16)],
        axis=0,
    )
    strip_ref[...] = silu(dot(we_ref[...], strip))


def rebuilt_kernel(mid_ref, edge_ref, halo_ref, strip_ref, ga_ref, out_ref, z_s, t_s, out_s):
    ga = ga_ref[...]
    zs = dot(ga, strip_ref[...])
    t0 = zs[:DEEP]
    t2 = zs[2 * DEEP : BAND]
    for a in (1, 2):
        t0 = t0 + pltpu.roll(zs[a * BAND : a * BAND + DEEP], LANES - 2 * a, 1)
        t2 = t2 + pltpu.roll(zs[a * BAND + 2 * DEEP : (a + 1) * BAND], LANES - 2 * a, 1)
    lane = lane_of((DEEP, LANES))
    even = lax.rem(lane, 2) == 0
    t_s[...] = jnp.where(even, pltpu.roll(t2, LANES - 1, 1), pltpu.roll(t0, 1, 1))

    def put(slot, first, second):
        z = dot(ga_ref[...], jnp.concatenate([first, second], axis=1))
        z_s[slot] = z[:, :LANES]
        z_s[slot + 1] = z[:, LANES:]

    put(0, halo_ref[0], edge_ref[0])
    for k in range(0, MID, 2):
        put(k + 2, mid_ref[k], mid_ref[k + 1])
    put(ROWS, edge_ref[1], halo_ref[1])

    for row in range(ROWS):
        sums = []
        for b in range(3):
            total = z_s[row, b * DEEP : (b + 1) * DEEP, :]
            for a in (1, 2):
                start = a * BAND + b * DEEP
                total = total + z_s[row + a, start : start + DEEP, :]
            sums.append(total)
        out = sums[1]
        out = out + jnp.where(lane == 0, 0.0, pltpu.roll(sums[0], 1, 1))
        out = out + jnp.where(lane == LANES - 1, 0.0, pltpu.roll(sums[2], LANES - 1, 1))
        side = pltpu.roll(t_s[...], LANES - 1 - 2 * row, 1)
        out = out + jnp.where((lane == 0) | (lane == LANES - 1), side, 0.0)
        out_s[pl.ds(row, DEEP, stride=ROWS), :] = out
    size = out_ref.shape[0] * ROWS
    out_ref[...] = out_s[:size, :].reshape(out_ref.shape).astype(BF16)


def turn_kernel(mid_ref, edge_ref, out_ref, out_s):
    rows = [edge_ref.at[0]] + [mid_ref.at[row] for row in range(MID)] + [edge_ref.at[1]]
    for row in range(ROWS):
        out_s[pl.ds(row, out_ref.shape[0], stride=ROWS), :] = rows[row][...].astype(F32)
    out_ref[...] = out_s[...].reshape(out_ref.shape).astype(BF16)


def total_kernel(pieces_ref, out_ref):
    total = pieces_ref[0].astype(F32)
    for k in range(1, pieces_ref.shape[0]):
        total = total + pieces_ref[k].astype(F32)
    total = total.astype(BF16)
    for k in range(out_ref.shape[0]):
        out_ref[k] = total


def final_kernel(norm, flags_ref, own_ref, other_ref, enc_ref, gen_ref, pack_s, out_s, sems):
    first = flags_ref[2] == 0
    own, other = own_ref[...].astype(F32), other_ref[...].astype(F32)
    pack_s[0] = jnp.where(first, own, other) * norm
    pack_s[1] = jnp.where(first, other, own) * norm
    copies = []
    for k, out in enumerate((gen_ref, enc_ref)):
        for group in range(3):
            for tap in range(3 * group, 3 * group + 3):
                out_s[k, tap, :, :LANES] = pack_s[k, 69 * tap : 69 * tap + 69, :]
                out_s[k, tap, :, LANES:] = pack_s[k, PACK + 69 * tap : PACK + 69 * tap + 69, :]
            taps = pl.ds(3 * group, 3)
            copies.append(
                pltpu.make_async_copy(out_s.at[k, taps], out.at[taps], sems.at[3 * k + group])
            )
            copies[-1].start()
    for copy in copies:
        copy.wait()


def swap_cores(value):
    return lax.ppermute(value, "core", [(0, 1), (1, 0)])


def great_circles(lat_count, lon_count):
    pairs = []
    for la in range(lat_count):
        for lo in range(lon_count):
            if lo < lon_count // 2:
                to = (la + 1, lo) if la < lat_count - 1 else (la, lo + lon_count // 2)
            else:
                to = (la - 1, lo) if la > 0 else (la, lo - lon_count // 2)
            pairs.append((la * lon_count + lo, to[0] * lon_count + to[1]))
    return pairs, [(b, a) for a, b in pairs]


def on_device(fields, enc_kernel, gen_kernel, recon_grad):
    variables, height, width = fields.shape
    channels = gen_kernel.shape[3]
    lat_index, lat_count = lax.axis_index(LAT), lax.axis_size(LAT)
    lon_count = lax.axis_size(LON)
    core = lax.axis_index("core")
    low = lax.axis_index("y_lo") == 0
    flags = jnp.stack(
        [
            (lat_index == 0).astype(jnp.int32),
            (lat_index == lat_count - 1).astype(jnp.int32),
            core.astype(jnp.int32),
            low.astype(jnp.int32),
        ]
    )
    pad = ((0, 0), (0, 0), (0, DEEP - variables), (0, 0))
    gen_rows = jnp.pad(gen_kernel, pad).reshape(TAPS, channels)
    enc_rows = jnp.pad(jnp.swapaxes(enc_kernel, 2, 3), pad).reshape(TAPS, channels)
    def shaped(*shape, dtype=BF16):
        return jax.ShapeDtypeStruct(shape, dtype)

    plane, side = shaped(ROWS, DEEP, LANES), shaped(SIDES // 2, ROWS * DEEP)
    x, r, east, west = call(
        columns_kernel,
        (plane, plane, side, side),
        10**7,
        [
            pltpu.VMEM(fields.shape, BF16),
            pltpu.VMEM(fields.shape, BF16),
            pltpu.VMEM((ROWS * DEEP, LANES), F32),
            pltpu.SemaphoreType.DMA((2,)),
        ],
    )(in_specs=[FAR] * 2, out_specs=(FULL,) * 4)(
        *(pltpu.with_memory_space_constraint(v, pltpu.HBM) for v in (fields, recon_grad))
    )
    right = [(i, (i + 1) % lon_count) for i in range(lon_count)]
    left = [(b, a) for a, b in right]
    east = lax.ppermute(east, LON, right)
    west = lax.ppermute(west, LON, left)
    packet = shaped(4, SENT, LANES)
    pa, pb = call(rows_kernel, (packet, packet), 10**7)(
        in_specs=[FLAGS] + [FULL] * 4, out_specs=(FULL,) * 2
    )(flags, x, r, east, west)
    ahead, behind = great_circles(lat_count, lon_count)
    pa = lax.ppermute(pa, LAT + LON, ahead)
    pb = lax.ppermute(pb, LAT + LON, behind)
    we, gt = enc_rows.T, gen_rows.T
    sums, packed = (2, TAPS, channels), (2 * PACK, LANES)
    few = shaped(4, BAND, LANES)
    feat_mid, hid_mid, acc, fe, re = call(
        inner_kernel,
        (
            shaped(MID, channels, LANES),
            shaped(MID, channels, LANES),
            shaped(*sums, dtype=F32),
            few,
            few,
        ),
        9 * 10**9,
        [
            pltpu.VMEM((ROWS, BAND, LANES), BF16),
            pltpu.VMEM((ROWS, BAND, LANES), BF16),
            pltpu.VMEM((MID, channels, LANES), BF16),
        ],
        16,
    )(in_specs=[FULL] * 6, out_specs=(FULL,) * 5)(x, r, east, west, we, gt)
    pair = shaped(2, channels, LANES)
    work = [pltpu.VMEM(sums[1:], F32), pltpu.VMEM((PACK + 8, channels), F32)]
    feat_edge, hid_edge, sent, lhs, rhs, poles = call(
        edge_kernel,
        (
            pair,
            pair,
            shaped(*packed),
            shaped(2, TAPS, 2 * LANES),
            shaped(2, channels, 2 * LANES),
            shaped(2, BAND, LANES),
        ),
        10**9,
        [pltpu.VMEM((2, BAND, LANES), BF16), pltpu.VMEM((2, BAND, LANES), BF16)] + work,
        16,
    )(in_specs=[FLAGS] + [FULL] * 7, out_specs=(FULL,) * 6)(
        flags, fe, re, pa, pb, we, gt, acc
    )
    kept = call(kept_kernel, shaped(*packed, dtype=F32), 10**9, work)(
        in_specs=[FLAGS] + [FULL] * 4, out_specs=FULL
    )(flags, acc, lhs, rhs, poles)
    half = (kept + swap_cores(sent).astype(F32)).astype(BF16)
    half, feat_edge, pa = lax.optimization_barrier((half, feat_edge, pa))
    halo, strip = call(
        beyond_kernel,
        (shaped(2, channels, LANES), shaped(channels, LANES)),
        10**9,
        [pltpu.VMEM((8, BAND, LANES), BF16), pltpu.VMEM((BAND, LANES), F32)],
    )(in_specs=[FLAGS] + [FULL] * 6, out_specs=(FULL,) * 2)(flags, x, east, west, pa, pb, we)
    rebuilt = call(
        rebuilt_kernel,
        shaped(variables, height, width),
        4 * 10**9,
        [
            pltpu.VMEM((ROWS + 2, TAPS, LANES), F32),
            pltpu.VMEM((DEEP, LANES), F32),
            pltpu.VMEM((DEEP * ROWS, LANES), F32),
        ],
        12,
    )(in_specs=[FULL] * 5, out_specs=FULL)(hid_mid, hid_edge, halo, strip, gen_rows)
    feat_grad = call(
        turn_kernel,
        shaped(channels, height, width),
        2 * 10**9,
        [pltpu.VMEM((channels * ROWS, LANES), F32)],
    )(in_specs=[FULL] * 2, out_specs=FULL)(feat_mid, feat_edge)

    faces, layers = lax.axis_size(FACE), lax.axis_size("z")
    piece = (2 * PACK // faces, LANES)

    def exchange(value, axes):
        return lax.all_to_all(value, axes, 0, 0, tiled=True)

    def total(pieces, copies):
        return call(total_kernel, jax.ShapeDtypeStruct((copies,) + piece, BF16), 10**7)(
            in_specs=[FULL], out_specs=FULL
        )(pieces)

    pieces = exchange(half.reshape((faces,) + piece), FACE)
    pieces, feat_grad, rebuilt = lax.optimization_barrier((pieces, feat_grad, rebuilt))
    pieces = exchange(total(pieces, layers), "z")
    own = exchange(total(pieces, faces), FACE).reshape(packed)
    other = swap_cores(own)
    norm = (height * lat_count * width * lon_count) ** -0.5
    grad = jax.ShapeDtypeStruct((9, variables, channels), F32)
    enc, gen = call(
        functools.partial(final_kernel, norm),
        (grad, grad),
        10**7,
        [
            pltpu.VMEM((2,) + packed, F32),
            pltpu.VMEM((2, 9, variables, channels), F32),
            pltpu.SemaphoreType.DMA((6,)),
        ],
    )(in_specs=[FLAGS, FULL, FULL], out_specs=(FAR, FAR))(flags, own, other)
    shape = (3, 3, variables, channels)
    return (rebuilt, feat_grad, jnp.swapaxes(enc.reshape(shape), 2, 3), gen.reshape(shape))


def solution(mesh):
    lat_count, lon_count = mesh.shape["lat"], mesh.shape["lon"]
    fine = Mesh(mesh.devices.reshape(lat_count // 2, 2, 2, lon_count // 4, 2), LAT + LON)
    return jax.shard_map(
        on_device,
        mesh=fine,
        in_specs=(P(None, LAT, LON), P(), P(), P(None, LAT, LON)),
        out_specs=(P(None, LAT, LON), P(None, LAT, LON), P(), P()),
        check_vma=False,
    )
```

```python
import functools

import jax
import jax.numpy as jnp
from jax import lax
from jax.experimental import pallas as pl
from jax.experimental.pallas import tpu as pltpu
from jax.sharding import Mesh
from jax.sharding import PartitionSpec as P

FACE = ("y_hi", "y_lo", "x")
LAT = ("z", "y_hi")
LON = ("y_lo", "x", "core")

LANES = 128
ROWS = 16
DEEP = 80
SENT = 72
SIDES = 16
MID = ROWS - 2
EDGES = (0, 1, ROWS - 2, ROWS - 1)
BAND = 3 * DEEP
TAPS = 3 * BAND
PACK = 640
F32 = jnp.float32
BF16 = jnp.bfloat16
NT = (((1,), (1,)), ((), ()))
TN = (((0,), (0,)), ((), ()))
FULL = pl.BlockSpec(memory_space=pltpu.VMEM)
FLAGS = pl.BlockSpec(memory_space=pltpu.SMEM)
FAR = pl.BlockSpec(memory_space=pltpu.HBM)


def lane_of(shape):
    return lax.broadcasted_iota(jnp.int32, shape, len(shape) - 1)


def dot(a, b, dims=(((1,), (0,)), ((), ()))):
    return lax.dot_general(a, b, dims, preferred_element_type=F32)


def call(kernel, outs, cost, scratch=(), limit=8):
    return functools.partial(
        pl.pallas_call,
        kernel,
        out_shape=outs,
        scratch_shapes=list(scratch),
        compiler_params=pltpu.CompilerParams(vmem_limit_bytes=limit << 20),
        cost_estimate=pl.CostEstimate(flops=cost, bytes_accessed=cost // 500, transcendentals=0),
    )


def picks(count, pairs):
    rows = lax.broadcasted_iota(jnp.int32, (SIDES, count), 0)
    lanes = lax.broadcasted_iota(jnp.int32, (SIDES, count), 1)
    hot = (rows == pairs[0][0]) & (lanes == pairs[0][1])
    for row, lane in pairs[1:]:
        hot = hot | ((rows == row) & (lanes == lane))
    return jnp.where(hot, 1.0, 0.0).astype(BF16)


def columns_kernel(
    fields_ref, cot_ref, enc_ref, gen_ref, x_ref, r_ref, east_ref, west_ref, er_ref, gr_ref,
    in_x, in_r, in_e, in_g, raw_s, sems,
):
    loads = [
        pltpu.make_async_copy(source, target, sems.at[k])
        for k, (source, target) in enumerate(
            ((fields_ref, in_x), (cot_ref, in_r), (enc_ref, in_e), (gen_ref, in_g))
        )
    ]
    for load in loads:
        load.start()
    size = in_x.shape[0] * ROWS
    sides = None
    for load, source, target, chosen in (
        (loads[0], in_x, x_ref, [(0, 126), (1, 127), (8, 0), (9, 1)]),
        (loads[1], in_r, r_ref, [(2, 127), (10, 0)]),
    ):
        load.wait()
        raw_s[:size, :] = source[...].astype(F32).reshape(size, LANES)
        raw_s[size:, :] = jnp.zeros((raw_s.shape[0] - size, LANES), F32)
        for row in range(ROWS):
            target[row] = raw_s[pl.ds(row, DEEP, stride=ROWS), :].astype(BF16)
        some = dot(picks(LANES, chosen), target[...].reshape(ROWS * DEEP, LANES), NT)
        sides = some if sides is None else sides + some
    for load, source, target in ((loads[2], in_e, er_ref), (loads[3], in_g, gr_ref)):
        load.wait()
        for tap in range(9):
            target[tap, 64:, :] = jnp.zeros((DEEP - 64, target.shape[2]), BF16)
            target[tap, : source.shape[1], :] = source[tap]
    east_ref[...] = sides[: SIDES // 2].astype(BF16)
    west_ref[...] = sides[SIDES // 2 :].astype(BF16)


def side_columns(east_ref, west_ref, rows):
    first, last = rows[0] * DEEP, (rows[-1] + 1) * DEEP
    east, west = east_ref[:, first:last].astype(F32), west_ref[:, first:last].astype(F32)
    return jnp.concatenate([east, west], axis=0).T.astype(BF16)


OWN = [(0, 126), (1, 127), (8, 0), (9, 1)]


def side_planes(columns):
    return dot(columns, picks(2 * LANES, OWN + [(2, LANES + 127), (10, LANES)]))


def rows_kernel(flags_ref, x_ref, r_ref, east_ref, west_ref, a_ref, b_ref):
    low = flags_ref[3] == 1
    edge_picks = picks(LANES, OWN + [(2, 7), (10, 8)])
    inner_picks = picks(LANES, [(0, 2), (1, 3), (8, 4), (9, 5)])

    def packet(edge, inner):
        both = side_columns(east_ref, west_ref, sorted((edge, inner)))
        outer, other = (both[:DEEP], both[DEEP:]) if edge < inner else (both[DEEP:], both[:DEEP])
        sides = dot(outer, edge_picks) + dot(other, inner_picks)
        return [x_ref[edge].astype(F32), x_ref[inner].astype(F32), r_ref[edge].astype(F32), sides]

    top, bottom = packet(0, 1), packet(ROWS - 1, ROWS - 2)
    for k in range(4):
        t, b = top[k][:SENT], bottom[k][:SENT]
        a_ref[k] = jnp.where(low, b, t).astype(BF16)
        b_ref[k] = jnp.where(low, t, b).astype(BF16)


def shifts(x, h):
    lane = lane_of(x.shape)
    left = pltpu.roll(jnp.where(lane == LANES - 1, h, x), 1, 1)
    right = pltpu.roll(jnp.where(lane == 0, h, x), LANES - 1, 1)
    return left, right


def put_field(ref, slot, x, h):
    left, right = shifts(x, h)
    ref[slot, :DEEP, :] = left.astype(BF16)
    ref[slot, DEEP : 2 * DEEP, :] = x.astype(BF16)
    ref[slot, 2 * DEEP :, :] = right.astype(BF16)


def put_cot(ref, slot, x, h):
    left, right = shifts(x, h)
    ref[slot, :DEEP, :] = right.astype(BF16)
    ref[slot, DEEP : 2 * DEEP, :] = x.astype(BF16)
    ref[slot, 2 * DEEP :, :] = left.astype(BF16)


def put_strip(ref, slot, x, h):
    lane = lane_of((DEEP, LANES))
    spot = 2 * slot
    hit = (lane == spot) | (lane == spot + 1)
    sides = (
        (jnp.where(lane == LANES - 1, x, h), spot + 2),
        (h, spot + 1),
        (jnp.where(lane == 0, x, h), spot),
    )
    for tap, (plane, turn) in enumerate(sides):
        rows = pl.ds(tap * DEEP, DEEP)
        ref[rows, :] = jnp.where(hit, pltpu.roll(plane, turn, 1), ref[rows, :])


def wide(ref, slots):
    return jnp.concatenate([ref[slot] for slot in slots], axis=1)


def stacks(ref, starts):
    return jnp.concatenate([ref[k : k + 3].reshape(TAPS, LANES) for k in starts], axis=1)


def inner_kernel(
    x_ref, r_ref, east_ref, west_ref, we_ref, gt_ref,
    feat_ref, hid_ref, acc_ref, fe_ref, re_ref, f_s, r_s, back_s,
):
    planes = side_planes(side_columns(east_ref, west_ref, range(ROWS)))
    for row in range(ROWS):
        side = planes[row * DEEP : (row + 1) * DEEP]
        put_field(f_s, row, x_ref[row].astype(F32), side[:, :LANES])
        put_cot(r_s, ROWS - 1 - row, r_ref[row].astype(F32), side[:, LANES:])
    for k, row in enumerate(EDGES):
        fe_ref[k] = f_s[row]
        re_ref[k] = r_s[ROWS - 1 - row]
    for k in range(0, MID, 2):
        pre = dot(we_ref[...], stacks(f_s, (k, k + 1)))
        gate = 1.0 / (1.0 + jnp.exp(-pre))
        hid = (pre * gate).astype(BF16)
        feat = dot(gt_ref[...], stacks(r_s, (MID - 1 - k, MID - 2 - k))).astype(BF16)
        back = (feat.astype(F32) * gate * (1.0 + pre * (1.0 - gate))).astype(BF16)
        for ref, value in ((feat_ref, feat), (hid_ref, hid), (back_s, back)):
            ref[k] = value[:, :LANES]
            ref[k + 1] = value[:, LANES:]
    rows = range(MID)
    acc_ref[0] = dot(stacks(r_s, [MID - 1 - k for k in rows]), wide(hid_ref, rows), NT)
    acc_ref[1] = dot(stacks(f_s, rows), wide(back_s, rows), NT)


def unpack(low, first_ref, second_ref):
    blank = jnp.zeros((DEEP - SENT, LANES), F32)
    cells = [
        jnp.concatenate(
            [jnp.where(low, first_ref[k].astype(F32), second_ref[k].astype(F32)), blank], axis=0
        )
        for k in range(4)
    ]
    return cells + [pltpu.roll(cells[3], LANES - turn, 1) for turn in (4, 8)]


def gradient(which, acc_ref, lhs_ref, rhs_ref, pole_ref, sum_s, pack_s, out_ref):
    sum_s[...] = acc_ref[which] + dot(lhs_ref[which], rhs_ref[which], NT)
    for k, start in ((0, 0), (1, 2 * BAND)):
        pole = jnp.where(which == 0, pole_ref[k].astype(F32), 0.0).astype(BF16)
        hid = rhs_ref[0, :, k * LANES : (k + 1) * LANES]
        sum_s[start : start + BAND, :] += dot(pole, hid, NT)
    for tap in range(9):
        pack_s[69 * tap : 69 * tap + 69, :] = sum_s[DEEP * tap : DEEP * tap + 69, :]
    pack_s[621:, :] = jnp.zeros((pack_s.shape[0] - 621, pack_s.shape[1]), F32)
    out_ref[:PACK, :] = pack_s[:PACK, :LANES].astype(out_ref.dtype)
    out_ref[PACK:, :] = pack_s[:PACK, LANES:].astype(out_ref.dtype)


def edge_kernel(
    flags_ref, fe_ref, re_ref, pa_ref, pb_ref, we_ref, gt_ref, acc_ref,
    feat_ref, hid_ref, sent_ref, lhs_ref, rhs_ref, pole_ref, out_s, cot_s, sum_s, pack_s,
):
    north, south = flags_ref[0] == 1, flags_ref[1] == 1
    core, low = flags_ref[2], flags_ref[3] == 1
    up, down = unpack(low, pa_ref, pb_ref), unpack(low, pb_ref, pa_ref)
    put_field(out_s, 0, up[0], up[3])
    put_field(out_s, 1, down[0], down[3])
    put_cot(cot_s, 0, jnp.where(north, 0.0, up[2]), jnp.where(north, 0.0, up[5]))
    put_cot(cot_s, 1, jnp.where(south, 0.0, down[2]), jnp.where(south, 0.0, down[5]))
    put_cot(pole_ref, 0, jnp.where(north, up[2], 0.0), jnp.where(north, up[5], 0.0))
    put_cot(pole_ref, 1, jnp.where(south, down[2], 0.0), jnp.where(south, down[5], 0.0))

    def beside(first, second):
        return jnp.concatenate(
            [jnp.concatenate(first, axis=0), jnp.concatenate(second, axis=0)], axis=1
        )

    lhs_ref[0] = beside(
        (re_ref[1], re_ref[0], cot_s[0]), (cot_s[1], re_ref[3], re_ref[2])
    )
    lhs_ref[1] = beside((out_s[0], fe_ref[0], fe_ref[1]), (fe_ref[2], fe_ref[3], out_s[1]))
    pre = dot(we_ref[...], lhs_ref[1])
    gate = 1.0 / (1.0 + jnp.exp(-pre))
    hid = (pre * gate).astype(BF16)
    extra = jnp.concatenate(
        [dot(gt_ref[:, :BAND], pole_ref[0]), dot(gt_ref[:, 2 * BAND :], pole_ref[1])], axis=1
    )
    feat = (dot(gt_ref[...], lhs_ref[0]) + extra).astype(BF16)
    back = (feat.astype(F32) * gate * (1.0 + pre * (1.0 - gate))).astype(BF16)
    hid_ref[0], hid_ref[1] = hid[:, :LANES], hid[:, LANES:]
    feat_ref[0], feat_ref[1] = feat[:, :LANES], feat[:, LANES:]
    rhs_ref[0], rhs_ref[1] = hid, back
    gradient(1 - core, acc_ref, lhs_ref, rhs_ref, pole_ref, sum_s, pack_s, sent_ref)


def kept_kernel(flags_ref, acc_ref, lhs_ref, rhs_ref, pole_ref, kept_ref, sum_s, pack_s):
    gradient(flags_ref[2], acc_ref, lhs_ref, rhs_ref, pole_ref, sum_s, pack_s, kept_ref)


def beyond_kernel(
    flags_ref, x_ref, east_ref, west_ref, pa_ref, pb_ref, we_ref, halo_ref, strip_ref, f_s, u_s
):
    north, south, low = flags_ref[0] == 1, flags_ref[1] == 1, flags_ref[3] == 1
    up, down = unpack(low, pa_ref, pb_ref), unpack(low, pb_ref, pa_ref)
    planes = side_planes(side_columns(east_ref, west_ref, range(ROWS)))
    u_s[...] = jnp.zeros_like(u_s)
    kept = {0: 2, 1: 3, ROWS - 2: 4, ROWS - 1: 5}
    for row in range(ROWS):
        x, h = x_ref[row].astype(F32), planes[row * DEEP : (row + 1) * DEEP, :LANES]
        put_strip(u_s, row + 2, x, h)
        if row in kept:
            put_field(f_s, kept[row], x, h)
    for slot, place, x, h in (
        (0, 0, up[1], up[4]),
        (1, 1, up[0], up[3]),
        (6, ROWS + 2, down[0], down[3]),
        (7, ROWS + 3, down[1], down[4]),
    ):
        put_field(f_s, slot, x, h)
        put_strip(u_s, place, x, h)

    def rows(flag, first, middle, last):
        a, c = f_s[first].astype(F32), f_s[last].astype(F32)
        ends = jnp.where(flag, c, a).astype(BF16), jnp.where(flag, a, c).astype(BF16)
        return jnp.concatenate([ends[0], f_s[middle], ends[1]], axis=0)

    def silu(v):
        return (v * (1.0 / (1.0 + jnp.exp(-v)))).astype(BF16)

    ring = jnp.concatenate([rows(north, 0, 1, 2), rows(south, 5, 6, 7)], axis=1)
    halo = silu(dot(we_ref[...], ring))
    halo_ref[0], halo_ref[1] = halo[:, :LANES], halo[:, LANES:]
    u = u_s[...]
    u2 = pltpu.roll(u, LANES - 2, 1)
    u4 = pltpu.roll(u, LANES - 4, 1)
    lane = lane_of(u.shape)
    last = 2 * (ROWS + 1)
    flip = (north & (lane < 2)) | (south & ((lane == last) | (lane == last + 1)))
    strip = jnp.concatenate(
        [jnp.where(flip, u4, u).astype(BF16), u2.astype(BF16), jnp.where(flip, u, u4).astype(BF16)],
        axis=0,
    )
    strip_ref[...] = silu(dot(we_ref[...], strip))


def rebuilt_kernel(mid_ref, edge_ref, halo_ref, strip_ref, ga_ref, out_ref, z_s, t_s, out_s):
    ga = ga_ref[...]
    zs = dot(ga, strip_ref[...])
    t0 = zs[:DEEP]
    t2 = zs[2 * DEEP : BAND]
    for a in (1, 2):
        t0 = t0 + pltpu.roll(zs[a * BAND : a * BAND + DEEP], LANES - 2 * a, 1)
        t2 = t2 + pltpu.roll(zs[a * BAND + 2 * DEEP : (a + 1) * BAND], LANES - 2 * a, 1)
    lane = lane_of((DEEP, LANES))
    even = lax.rem(lane, 2) == 0
    t_s[...] = jnp.where(even, pltpu.roll(t2, LANES - 1, 1), pltpu.roll(t0, 1, 1))

    def put(slot, first, second):
        z = dot(ga_ref[...], jnp.concatenate([first, second], axis=1))
        z_s[slot] = z[:, :LANES]
        z_s[slot + 1] = z[:, LANES:]

    put(0, halo_ref[0], edge_ref[0])
    for k in range(0, MID, 2):
        put(k + 2, mid_ref[k], mid_ref[k + 1])
    put(ROWS, edge_ref[1], halo_ref[1])

    for row in range(ROWS):
        sums = []
        for b in range(3):
            total = z_s[row, b * DEEP : (b + 1) * DEEP, :]
            for a in (1, 2):
                start = a * BAND + b * DEEP
                total = total + z_s[row + a, start : start + DEEP, :]
            sums.append(total)
        out = sums[1]
        out = out + jnp.where(lane == 0, 0.0, pltpu.roll(sums[0], 1, 1))
        out = out + jnp.where(lane == LANES - 1, 0.0, pltpu.roll(sums[2], LANES - 1, 1))
        side = pltpu.roll(t_s[...], LANES - 1 - 2 * row, 1)
        out = out + jnp.where((lane == 0) | (lane == LANES - 1), side, 0.0)
        out_s[pl.ds(row, DEEP, stride=ROWS), :] = out
    size = out_ref.shape[0] * ROWS
    out_ref[...] = out_s[:size, :].reshape(out_ref.shape).astype(BF16)


def turn_kernel(part, mid_ref, edge_ref, *refs):
    into_ref, out_s, turned_s, sem = refs[-4:]
    count = turned_s.shape[0]
    chosen = pl.ds(part * count, count)
    for row in range(ROWS):
        source = mid_ref.at[row - 1] if 0 < row <= MID else edge_ref.at[min(row, 1)]
        out_s[pl.ds(row, count, stride=ROWS), :] = source[chosen, :].astype(F32)
    turned_s[...] = out_s[...].reshape(turned_s.shape).astype(BF16)
    copy = pltpu.make_async_copy(turned_s, into_ref.at[chosen], sem)
    copy.start()
    copy.wait()


def total_kernel(pieces_ref, out_ref):
    total = pieces_ref[0].astype(F32)
    for k in range(1, pieces_ref.shape[0]):
        total = total + pieces_ref[k].astype(F32)
    total = total.astype(BF16)
    for k in range(out_ref.shape[0]):
        out_ref[k] = total


def final_kernel(norm, flags_ref, own_ref, other_ref, enc_ref, gen_ref, pack_s, out_s, sems):
    first = flags_ref[2] == 0
    own, other = own_ref[...].astype(F32), other_ref[...].astype(F32)
    copies = []
    for k, out in enumerate((gen_ref, enc_ref)):
        pack_s[k] = (jnp.where(first, other, own) if k else jnp.where(first, own, other)) * norm
        for group in range(3):
            for tap in range(3 * group, 3 * group + 3):
                out_s[k, tap, :, :LANES] = pack_s[k, 69 * tap : 69 * tap + 69, :]
                out_s[k, tap, :, LANES:] = pack_s[k, PACK + 69 * tap : PACK + 69 * tap + 69, :]
            taps = pl.ds(3 * group, 3)
            copies.append(
                pltpu.make_async_copy(out_s.at[k, taps], out.at[taps], sems.at[3 * k + group])
            )
            copies[-1].start()
    for copy in copies:
        copy.wait()


def swap_cores(value):
    return lax.ppermute(value, "core", [(0, 1), (1, 0)])


def great_circles(lat_count, lon_count):
    pairs = []
    for la in range(lat_count):
        for lo in range(lon_count):
            if lo < lon_count // 2:
                to = (la + 1, lo) if la < lat_count - 1 else (la, lo + lon_count // 2)
            else:
                to = (la - 1, lo) if la > 0 else (la, lo - lon_count // 2)
            pairs.append((la * lon_count + lo, to[0] * lon_count + to[1]))
    return pairs, [(b, a) for a, b in pairs]


def on_device(fields, enc_kernel, gen_kernel, recon_grad):
    variables, height, width = fields.shape
    channels = gen_kernel.shape[3]
    lat_index, lat_count = lax.axis_index(LAT), lax.axis_size(LAT)
    lon_count = lax.axis_size(LON)
    core = lax.axis_index("core")
    low = lax.axis_index("y_lo") == 0
    flags = jnp.stack(
        [
            (lat_index == 0).astype(jnp.int32),
            (lat_index == lat_count - 1).astype(jnp.int32),
            core.astype(jnp.int32),
            low.astype(jnp.int32),
        ]
    )
    def shaped(*shape, dtype=BF16):
        return jax.ShapeDtypeStruct(shape, dtype)

    plane, side = shaped(ROWS, DEEP, LANES), shaped(SIDES // 2, ROWS * DEEP)
    weights = shaped(9, DEEP, channels)
    taps = (9, variables, channels)
    x, r, east, west, enc_rows, gen_rows = call(
        columns_kernel,
        (plane, plane, side, side, weights, weights),
        10**7,
        [
            pltpu.VMEM(fields.shape, BF16),
            pltpu.VMEM(fields.shape, BF16),
            pltpu.VMEM(taps, BF16),
            pltpu.VMEM(taps, BF16),
            pltpu.VMEM((ROWS * DEEP, LANES), F32),
            pltpu.SemaphoreType.DMA((4,)),
        ],
    )(in_specs=[FAR] * 4, out_specs=(FULL,) * 6)(
        *(
            pltpu.with_memory_space_constraint(v, pltpu.HBM)
            for v in (
                fields,
                recon_grad,
                jnp.swapaxes(enc_kernel, 2, 3).reshape(taps),
                gen_kernel.reshape(taps),
            )
        )
    )
    enc_rows, gen_rows = (v.reshape(TAPS, channels) for v in (enc_rows, gen_rows))
    right = [(i, (i + 1) % lon_count) for i in range(lon_count)]
    left = [(b, a) for a, b in right]
    east = lax.ppermute(east, LON, right)
    west = lax.ppermute(west, LON, left)
    packet = shaped(4, SENT, LANES)
    pa, pb = call(rows_kernel, (packet, packet), 10**7)(
        in_specs=[FLAGS] + [FULL] * 4, out_specs=(FULL,) * 2
    )(flags, x, r, east, west)
    ahead, behind = great_circles(lat_count, lon_count)
    pa = lax.ppermute(pa, LAT + LON, ahead)
    pb = lax.ppermute(pb, LAT + LON, behind)
    we, gt = enc_rows.T, gen_rows.T
    sums, packed = (2, TAPS, channels), (2 * PACK, LANES)
    few = shaped(4, BAND, LANES)
    feat_mid, hid_mid, acc, fe, re = call(
        inner_kernel,
        (
            shaped(MID, channels, LANES),
            shaped(MID, channels, LANES),
            shaped(*sums, dtype=F32),
            few,
            few,
        ),
        9 * 10**9,
        [
            pltpu.VMEM((ROWS, BAND, LANES), BF16),
            pltpu.VMEM((ROWS, BAND, LANES), BF16),
            pltpu.VMEM((MID, channels, LANES), BF16),
        ],
        16,
    )(in_specs=[FULL] * 6, out_specs=(FULL,) * 5)(x, r, east, west, we, gt)
    pair = shaped(2, channels, LANES)
    work = [pltpu.VMEM(sums[1:], F32), pltpu.VMEM((PACK + 8, channels), F32)]
    feat_edge, hid_edge, sent, lhs, rhs, poles = call(
        edge_kernel,
        (
            pair,
            pair,
            shaped(*packed),
            shaped(2, TAPS, 2 * LANES),
            shaped(2, channels, 2 * LANES),
            shaped(2, BAND, LANES),
        ),
        10**9,
        [pltpu.VMEM((2, BAND, LANES), BF16), pltpu.VMEM((2, BAND, LANES), BF16)] + work,
        16,
    )(in_specs=[FLAGS] + [FULL] * 7, out_specs=(FULL,) * 6)(
        flags, fe, re, pa, pb, we, gt, acc
    )
    kept = call(kept_kernel, shaped(*packed, dtype=F32), 10**9, work)(
        in_specs=[FLAGS] + [FULL] * 4, out_specs=FULL
    )(flags, acc, lhs, rhs, poles)
    half = (kept + swap_cores(sent).astype(F32)).astype(BF16)
    half, feat_edge, pa = lax.optimization_barrier((half, feat_edge, pa))
    halo, strip = call(
        beyond_kernel,
        (shaped(2, channels, LANES), shaped(channels, LANES)),
        10**9,
        [pltpu.VMEM((8, BAND, LANES), BF16), pltpu.VMEM((BAND, LANES), F32)],
    )(in_specs=[FLAGS] + [FULL] * 6, out_specs=(FULL,) * 2)(flags, x, east, west, pa, pb, we)
    rebuilt = call(
        rebuilt_kernel,
        shaped(variables, height, width),
        4 * 10**9,
        [
            pltpu.VMEM((ROWS + 2, TAPS, LANES), F32),
            pltpu.VMEM((DEEP, LANES), F32),
            pltpu.VMEM((DEEP * ROWS, LANES), F32),
        ],
        12,
    )(in_specs=[FULL] * 5, out_specs=FULL)(hid_mid, hid_edge, halo, strip, gen_rows)

    def turn(part, *earlier):
        half_channels = channels // 2
        return pl.pallas_call(
            functools.partial(turn_kernel, part),
            out_shape=shaped(channels, height, width),
            in_specs=[FULL] * 2 + [FAR] * len(earlier),
            out_specs=FAR,
            scratch_shapes=[
                pltpu.VMEM((half_channels * ROWS, LANES), F32),
                pltpu.VMEM((half_channels, height, width), BF16),
                pltpu.SemaphoreType.DMA,
            ],
            input_output_aliases={2: 0} if earlier else {},
            compiler_params=pltpu.CompilerParams(vmem_limit_bytes=8 << 20),
            cost_estimate=pl.CostEstimate(flops=10**9, bytes_accessed=10**6, transcendentals=0),
        )(feat_mid, feat_edge, *earlier)

    feat_grad = turn(0)
    faces, layers = lax.axis_size(FACE), lax.axis_size("z")
    piece = (2 * PACK // faces, LANES)

    def exchange(value, axes):
        return lax.all_to_all(value, axes, 0, 0, tiled=True)

    def total(pieces, copies):
        return call(total_kernel, jax.ShapeDtypeStruct((copies,) + piece, BF16), 10**7)(
            in_specs=[FULL], out_specs=FULL
        )(pieces)

    pieces = exchange(half.reshape((faces,) + piece), FACE)
    pieces, feat_grad, rebuilt = lax.optimization_barrier((pieces, feat_grad, rebuilt))
    pieces = exchange(total(pieces, layers), "z")
    own = exchange(total(pieces, faces), FACE).reshape(packed)
    own, feat_mid, feat_edge, feat_grad = lax.optimization_barrier(
        (own, feat_mid, feat_edge, feat_grad)
    )
    other = swap_cores(own)
    feat_grad = turn(1, feat_grad)
    norm = (height * lat_count * width * lon_count) ** -0.5
    grad = jax.ShapeDtypeStruct((9, variables, channels), F32)
    enc, gen = call(
        functools.partial(final_kernel, norm),
        (grad, grad),
        10**7,
        [
            pltpu.VMEM((2,) + packed, F32),
            pltpu.VMEM((2, 9, variables, channels), F32),
            pltpu.SemaphoreType.DMA((6,)),
        ],
    )(in_specs=[FLAGS, FULL, FULL], out_specs=(FAR, FAR))(flags, own, other)
    shape = (3, 3, variables, channels)
    return (rebuilt, feat_grad, jnp.swapaxes(enc.reshape(shape), 2, 3), gen.reshape(shape))


def solution(mesh):
    lat_count, lon_count = mesh.shape["lat"], mesh.shape["lon"]
    fine = Mesh(mesh.devices.reshape(lat_count // 2, 2, 2, lon_count // 4, 2), LAT + LON)
    return jax.shard_map(
        on_device,
        mesh=fine,
        in_specs=(P(None, LAT, LON), P(), P(), P(None, LAT, LON)),
        out_specs=(P(None, LAT, LON), P(None, LAT, LON), P(), P()),
        check_vma=False,
    )
```

```python
import functools

import jax
import jax.numpy as jnp
from jax import lax
from jax.experimental import pallas as pl
from jax.experimental.pallas import tpu as pltpu
from jax.sharding import Mesh
from jax.sharding import PartitionSpec as P

FACE = ("y_hi", "y_lo", "x")
LAT = ("z", "y_hi")
LON = ("y_lo", "x", "core")

LANES = 128
ROWS = 16
DEEP = 80
SENT = 72
SIDES = 16
MID = ROWS - 2
EDGES = (0, 1, ROWS - 2, ROWS - 1)
BAND = 3 * DEEP
TAPS = 3 * BAND
PACK = 640
F32 = jnp.float32
BF16 = jnp.bfloat16
NT = (((1,), (1,)), ((), ()))
TN = (((0,), (0,)), ((), ()))
FULL = pl.BlockSpec(memory_space=pltpu.VMEM)
FLAGS = pl.BlockSpec(memory_space=pltpu.SMEM)
FAR = pl.BlockSpec(memory_space=pltpu.HBM)


def lane_of(shape):
    return lax.broadcasted_iota(jnp.int32, shape, len(shape) - 1)


def dot(a, b, dims=(((1,), (0,)), ((), ()))):
    return lax.dot_general(a, b, dims, preferred_element_type=F32)


def call(kernel, outs, cost, scratch=(), limit=8):
    return functools.partial(
        pl.pallas_call,
        kernel,
        out_shape=outs,
        scratch_shapes=list(scratch),
        compiler_params=pltpu.CompilerParams(vmem_limit_bytes=limit << 20),
        cost_estimate=pl.CostEstimate(flops=cost, bytes_accessed=cost // 500, transcendentals=0),
    )


def picks(count, pairs):
    rows = lax.broadcasted_iota(jnp.int32, (SIDES, count), 0)
    lanes = lax.broadcasted_iota(jnp.int32, (SIDES, count), 1)
    hot = (rows == pairs[0][0]) & (lanes == pairs[0][1])
    for row, lane in pairs[1:]:
        hot = hot | ((rows == row) & (lanes == lane))
    return jnp.where(hot, 1.0, 0.0).astype(BF16)


def columns_kernel(
    fields_ref, cot_ref, enc_ref, gen_ref, x_ref, r_ref, we_ref, wg_ref, east_ref, west_ref, sems
):
    loads = [
        pltpu.make_async_copy(source, target, sems.at[k])
        for k, (source, target) in enumerate(
            ((fields_ref, x_ref), (cot_ref, r_ref), (enc_ref, we_ref), (gen_ref, wg_ref))
        )
    ]
    for load in loads:
        load.start()
    sides = None
    for load, source, chosen in (
        (loads[0], x_ref, [(0, 126), (1, 127), (8, 0), (9, 1)]),
        (loads[1], r_ref, [(2, 127), (10, 0)]),
    ):
        load.wait()
        cells = source[...].reshape(source.shape[0] * ROWS, LANES)
        some = dot(picks(LANES, chosen), cells, NT)
        sides = some if sides is None else sides + some
    east_ref[...] = sides[: SIDES // 2].astype(BF16)
    west_ref[...] = sides[SIDES // 2 :].astype(BF16)
    loads[2].wait()
    loads[3].wait()


def planes_kernel(fields_ref, cot_ref, enc_ref, gen_ref, x_ref, r_ref, er_ref, gr_ref, raw_s):
    size = fields_ref.shape[0] * ROWS
    raw_s[size:, :] = jnp.zeros((raw_s.shape[0] - size, LANES), F32)
    for source, target in ((fields_ref, x_ref), (cot_ref, r_ref)):
        raw_s[:size, :] = source[...].astype(F32).reshape(size, LANES)
        for row in range(ROWS):
            target[row] = raw_s[pl.ds(row, DEEP, stride=ROWS), :].astype(BF16)
    for source, target in ((enc_ref, er_ref), (gen_ref, gr_ref)):
        for tap in range(9):
            target[tap, 64:, :] = jnp.zeros((DEEP - 64, target.shape[2]), BF16)
            target[tap, : source.shape[1], :] = source[tap]


def side_columns(east_ref, west_ref, turn_s):
    size = east_ref.shape[1]
    both = jnp.concatenate([east_ref[...].astype(F32), west_ref[...].astype(F32)], axis=0)
    turn_s[:size, :] = both.T
    turn_s[size:, :] = jnp.zeros((turn_s.shape[0] - size, SIDES), F32)

    def of(rows):
        return jnp.concatenate(
            [turn_s[pl.ds(row, DEEP, stride=ROWS), :] for row in rows], axis=0
        ).astype(BF16)

    return of


OWN = [(0, 126), (1, 127), (8, 0), (9, 1)]


def side_planes(columns):
    return dot(columns, picks(2 * LANES, OWN + [(2, LANES + 127), (10, LANES)]))


def rows_kernel(flags_ref, x_ref, r_ref, east_ref, west_ref, a_ref, b_ref, turn_s):
    columns = side_columns(east_ref, west_ref, turn_s)
    low = flags_ref[3] == 1
    edge_picks = picks(LANES, OWN + [(2, 7), (10, 8)])
    inner_picks = picks(LANES, [(0, 2), (1, 3), (8, 4), (9, 5)])

    def packet(edge, inner):
        sides = dot(columns([edge]), edge_picks) + dot(columns([inner]), inner_picks)
        return [x_ref[edge].astype(F32), x_ref[inner].astype(F32), r_ref[edge].astype(F32), sides]

    top, bottom = packet(0, 1), packet(ROWS - 1, ROWS - 2)
    for k in range(4):
        t, b = top[k][:SENT], bottom[k][:SENT]
        a_ref[k] = jnp.where(low, b, t).astype(BF16)
        b_ref[k] = jnp.where(low, t, b).astype(BF16)


def shifts(x, h):
    lane = lane_of(x.shape)
    left = pltpu.roll(jnp.where(lane == LANES - 1, h, x), 1, 1)
    right = pltpu.roll(jnp.where(lane == 0, h, x), LANES - 1, 1)
    return left, right


def put_field(ref, slot, x, h):
    left, right = shifts(x, h)
    ref[slot, :DEEP, :] = left.astype(BF16)
    ref[slot, DEEP : 2 * DEEP, :] = x.astype(BF16)
    ref[slot, 2 * DEEP :, :] = right.astype(BF16)


def put_cot(ref, slot, x, h):
    left, right = shifts(x, h)
    ref[slot, :DEEP, :] = right.astype(BF16)
    ref[slot, DEEP : 2 * DEEP, :] = x.astype(BF16)
    ref[slot, 2 * DEEP :, :] = left.astype(BF16)


def put_strip(ref, slot, x, h):
    lane = lane_of((DEEP, LANES))
    spot = 2 * slot
    hit = (lane == spot) | (lane == spot + 1)
    sides = (
        (jnp.where(lane == LANES - 1, x, h), spot + 2),
        (h, spot + 1),
        (jnp.where(lane == 0, x, h), spot),
    )
    for tap, (plane, turn) in enumerate(sides):
        rows = pl.ds(tap * DEEP, DEEP)
        ref[rows, :] = jnp.where(hit, pltpu.roll(plane, turn, 1), ref[rows, :])


def wide(ref, slots):
    return jnp.concatenate([ref[slot] for slot in slots], axis=1)


def stacks(ref, starts):
    return jnp.concatenate([ref[k : k + 3].reshape(TAPS, LANES) for k in starts], axis=1)


def inner_kernel(
    x_ref, r_ref, east_ref, west_ref, we_ref, gt_ref,
    feat_ref, hid_ref, acc_ref, fe_ref, re_ref, f_s, r_s, back_s, turn_s,
):
    planes = side_planes(side_columns(east_ref, west_ref, turn_s)(range(ROWS)))
    for row in range(ROWS):
        side = planes[row * DEEP : (row + 1) * DEEP]
        put_field(f_s, row, x_ref[row].astype(F32), side[:, :LANES])
        put_cot(r_s, ROWS - 1 - row, r_ref[row].astype(F32), side[:, LANES:])
    for k, row in enumerate(EDGES):
        fe_ref[k] = f_s[row]
        re_ref[k] = r_s[ROWS - 1 - row]
    for k in range(0, MID, 2):
        pre = dot(we_ref[...], stacks(f_s, (k, k + 1)))
        gate = 1.0 / (1.0 + jnp.exp(-pre))
        hid = (pre * gate).astype(BF16)
        feat = dot(gt_ref[...], stacks(r_s, (MID - 1 - k, MID - 2 - k))).astype(BF16)
        back = (feat.astype(F32) * gate * (1.0 + pre * (1.0 - gate))).astype(BF16)
        for ref, value in ((feat_ref, feat), (hid_ref, hid), (back_s, back)):
            ref[k] = value[:, :LANES]
            ref[k + 1] = value[:, LANES:]
    rows = range(MID)
    acc_ref[0] = dot(stacks(r_s, [MID - 1 - k for k in rows]), wide(hid_ref, rows), NT)
    acc_ref[1] = dot(stacks(f_s, rows), wide(back_s, rows), NT)


def unpack(low, first_ref, second_ref):
    blank = jnp.zeros((DEEP - SENT, LANES), F32)
    cells = [
        jnp.concatenate(
            [jnp.where(low, first_ref[k].astype(F32), second_ref[k].astype(F32)), blank], axis=0
        )
        for k in range(4)
    ]
    return cells + [pltpu.roll(cells[3], LANES - turn, 1) for turn in (4, 8)]


def gradient(which, acc_ref, lhs_ref, rhs_ref, pole_ref, sum_s, pack_s, out_ref):
    sum_s[...] = acc_ref[which] + dot(lhs_ref[which], rhs_ref[which], NT)
    for k, start in ((0, 0), (1, 2 * BAND)):
        pole = jnp.where(which == 0, pole_ref[k].astype(F32), 0.0).astype(BF16)
        hid = rhs_ref[0, :, k * LANES : (k + 1) * LANES]
        sum_s[start : start + BAND, :] += dot(pole, hid, NT)
    for tap in range(9):
        pack_s[69 * tap : 69 * tap + 69, :] = sum_s[DEEP * tap : DEEP * tap + 69, :]
    pack_s[621:, :] = jnp.zeros((pack_s.shape[0] - 621, pack_s.shape[1]), F32)
    out_ref[:PACK, :] = pack_s[:PACK, :LANES].astype(out_ref.dtype)
    out_ref[PACK:, :] = pack_s[:PACK, LANES:].astype(out_ref.dtype)


def edge_kernel(
    flags_ref, fe_ref, re_ref, pa_ref, pb_ref, we_ref, gt_ref, acc_ref,
    feat_ref, hid_ref, sent_ref, lhs_ref, rhs_ref, pole_ref, out_s, cot_s, sum_s, pack_s,
):
    north, south = flags_ref[0] == 1, flags_ref[1] == 1
    core, low = flags_ref[2], flags_ref[3] == 1
    up, down = unpack(low, pa_ref, pb_ref), unpack(low, pb_ref, pa_ref)
    put_field(out_s, 0, up[0], up[3])
    put_field(out_s, 1, down[0], down[3])
    put_cot(cot_s, 0, jnp.where(north, 0.0, up[2]), jnp.where(north, 0.0, up[5]))
    put_cot(cot_s, 1, jnp.where(south, 0.0, down[2]), jnp.where(south, 0.0, down[5]))
    put_cot(pole_ref, 0, jnp.where(north, up[2], 0.0), jnp.where(north, up[5], 0.0))
    put_cot(pole_ref, 1, jnp.where(south, down[2], 0.0), jnp.where(south, down[5], 0.0))

    def beside(first, second):
        return jnp.concatenate(
            [jnp.concatenate(first, axis=0), jnp.concatenate(second, axis=0)], axis=1
        )

    lhs_ref[0] = beside(
        (re_ref[1], re_ref[0], cot_s[0]), (cot_s[1], re_ref[3], re_ref[2])
    )
    lhs_ref[1] = beside((out_s[0], fe_ref[0], fe_ref[1]), (fe_ref[2], fe_ref[3], out_s[1]))
    pre = dot(we_ref[...], lhs_ref[1])
    gate = 1.0 / (1.0 + jnp.exp(-pre))
    hid = (pre * gate).astype(BF16)
    extra = jnp.concatenate(
        [dot(gt_ref[:, :BAND], pole_ref[0]), dot(gt_ref[:, 2 * BAND :], pole_ref[1])], axis=1
    )
    feat = (dot(gt_ref[...], lhs_ref[0]) + extra).astype(BF16)
    back = (feat.astype(F32) * gate * (1.0 + pre * (1.0 - gate))).astype(BF16)
    hid_ref[0], hid_ref[1] = hid[:, :LANES], hid[:, LANES:]
    feat_ref[0], feat_ref[1] = feat[:, :LANES], feat[:, LANES:]
    rhs_ref[0], rhs_ref[1] = hid, back
    gradient(1 - core, acc_ref, lhs_ref, rhs_ref, pole_ref, sum_s, pack_s, sent_ref)


def kept_kernel(flags_ref, acc_ref, lhs_ref, rhs_ref, pole_ref, kept_ref, sum_s, pack_s):
    gradient(flags_ref[2], acc_ref, lhs_ref, rhs_ref, pole_ref, sum_s, pack_s, kept_ref)


def beyond_kernel(
    flags_ref, x_ref, east_ref, west_ref, pa_ref, pb_ref, we_ref,
    halo_ref, strip_ref, f_s, u_s, turn_s,
):
    north, south, low = flags_ref[0] == 1, flags_ref[1] == 1, flags_ref[3] == 1
    up, down = unpack(low, pa_ref, pb_ref), unpack(low, pb_ref, pa_ref)
    planes = side_planes(side_columns(east_ref, west_ref, turn_s)(range(ROWS)))
    u_s[...] = jnp.zeros_like(u_s)
    kept = {0: 2, 1: 3, ROWS - 2: 4, ROWS - 1: 5}
    for row in range(ROWS):
        x, h = x_ref[row].astype(F32), planes[row * DEEP : (row + 1) * DEEP, :LANES]
        put_strip(u_s, row + 2, x, h)
        if row in kept:
            put_field(f_s, kept[row], x, h)
    for slot, place, x, h in (
        (0, 0, up[1], up[4]),
        (1, 1, up[0], up[3]),
        (6, ROWS + 2, down[0], down[3]),
        (7, ROWS + 3, down[1], down[4]),
    ):
        put_field(f_s, slot, x, h)
        put_strip(u_s, place, x, h)

    def rows(flag, first, middle, last):
        a, c = f_s[first].astype(F32), f_s[last].astype(F32)
        ends = jnp.where(flag, c, a).astype(BF16), jnp.where(flag, a, c).astype(BF16)
        return jnp.concatenate([ends[0], f_s[middle], ends[1]], axis=0)

    def silu(v):
        return (v * (1.0 / (1.0 + jnp.exp(-v)))).astype(BF16)

    ring = jnp.concatenate([rows(north, 0, 1, 2), rows(south, 5, 6, 7)], axis=1)
    halo = silu(dot(we_ref[...], ring))
    halo_ref[0], halo_ref[1] = halo[:, :LANES], halo[:, LANES:]
    u = u_s[...]
    u2 = pltpu.roll(u, LANES - 2, 1)
    u4 = pltpu.roll(u, LANES - 4, 1)
    lane = lane_of(u.shape)
    last = 2 * (ROWS + 1)
    flip = (north & (lane < 2)) | (south & ((lane == last) | (lane == last + 1)))
    strip = jnp.concatenate(
        [jnp.where(flip, u4, u).astype(BF16), u2.astype(BF16), jnp.where(flip, u, u4).astype(BF16)],
        axis=0,
    )
    strip_ref[...] = silu(dot(we_ref[...], strip))


def rebuilt_kernel(mid_ref, edge_ref, halo_ref, strip_ref, ga_ref, out_ref, z_s, t_s, out_s):
    ga = ga_ref[...]
    zs = dot(ga, strip_ref[...])
    t0 = zs[:DEEP]
    t2 = zs[2 * DEEP : BAND]
    for a in (1, 2):
        t0 = t0 + pltpu.roll(zs[a * BAND : a * BAND + DEEP], LANES - 2 * a, 1)
        t2 = t2 + pltpu.roll(zs[a * BAND + 2 * DEEP : (a + 1) * BAND], LANES - 2 * a, 1)
    lane = lane_of((DEEP, LANES))
    even = lax.rem(lane, 2) == 0
    t_s[...] = jnp.where(even, pltpu.roll(t2, LANES - 1, 1), pltpu.roll(t0, 1, 1))

    def put(slot, first, second):
        z = dot(ga_ref[...], jnp.concatenate([first, second], axis=1))
        z_s[slot] = z[:, :LANES]
        z_s[slot + 1] = z[:, LANES:]

    put(0, halo_ref[0], edge_ref[0])
    for k in range(0, MID, 2):
        put(k + 2, mid_ref[k], mid_ref[k + 1])
    put(ROWS, edge_ref[1], halo_ref[1])

    for row in range(ROWS):
        sums = []
        for b in range(3):
            total = z_s[row, b * DEEP : (b + 1) * DEEP, :]
            for a in (1, 2):
                start = a * BAND + b * DEEP
                total = total + z_s[row + a, start : start + DEEP, :]
            sums.append(total)
        out = sums[1]
        out = out + jnp.where(lane == 0, 0.0, pltpu.roll(sums[0], 1, 1))
        out = out + jnp.where(lane == LANES - 1, 0.0, pltpu.roll(sums[2], LANES - 1, 1))
        side = pltpu.roll(t_s[...], LANES - 1 - 2 * row, 1)
        out = out + jnp.where((lane == 0) | (lane == LANES - 1), side, 0.0)
        out_s[pl.ds(row, DEEP, stride=ROWS), :] = out
    size = out_ref.shape[0] * ROWS
    out_ref[...] = out_s[:size, :].reshape(out_ref.shape).astype(BF16)


def turn_kernel(part, mid_ref, edge_ref, *refs):
    into_ref, out_s, turned_s, sem = refs[-4:]
    count = turned_s.shape[0]
    chosen = pl.ds(part * count, count)
    for row in range(ROWS):
        source = mid_ref.at[row - 1] if 0 < row <= MID else edge_ref.at[min(row, 1)]
        out_s[pl.ds(row, count, stride=ROWS), :] = source[chosen, :].astype(F32)
    turned_s[...] = out_s[...].reshape(turned_s.shape).astype(BF16)
    copy = pltpu.make_async_copy(turned_s, into_ref.at[chosen], sem)
    copy.start()
    copy.wait()


def total_kernel(pieces_ref, out_ref):
    total = pieces_ref[0].astype(F32)
    for k in range(1, pieces_ref.shape[0]):
        total = total + pieces_ref[k].astype(F32)
    total = total.astype(BF16)
    for k in range(out_ref.shape[0]):
        out_ref[k] = total


def final_kernel(norm, flags_ref, own_ref, other_ref, enc_ref, gen_ref, pack_s, out_s, sems):
    first = flags_ref[2] == 0
    own, other = own_ref[...].astype(F32), other_ref[...].astype(F32)
    copies = []
    for k, out in enumerate((gen_ref, enc_ref)):
        pack_s[k] = (jnp.where(first, other, own) if k else jnp.where(first, own, other)) * norm
        for group in range(3):
            for tap in range(3 * group, 3 * group + 3):
                out_s[k, tap, :, :LANES] = pack_s[k, 69 * tap : 69 * tap + 69, :]
                out_s[k, tap, :, LANES:] = pack_s[k, PACK + 69 * tap : PACK + 69 * tap + 69, :]
            taps = pl.ds(3 * group, 3)
            copies.append(
                pltpu.make_async_copy(out_s.at[k, taps], out.at[taps], sems.at[3 * k + group])
            )
            copies[-1].start()
    for copy in copies:
        copy.wait()


def swap_cores(value):
    return lax.ppermute(value, "core", [(0, 1), (1, 0)])


def great_circles(lat_count, lon_count):
    pairs = []
    for la in range(lat_count):
        for lo in range(lon_count):
            if lo < lon_count // 2:
                to = (la + 1, lo) if la < lat_count - 1 else (la, lo + lon_count // 2)
            else:
                to = (la - 1, lo) if la > 0 else (la, lo - lon_count // 2)
            pairs.append((la * lon_count + lo, to[0] * lon_count + to[1]))
    return pairs, [(b, a) for a, b in pairs]


def on_device(fields, enc_kernel, gen_kernel, recon_grad):
    variables, height, width = fields.shape
    channels = gen_kernel.shape[3]
    lat_index, lat_count = lax.axis_index(LAT), lax.axis_size(LAT)
    lon_count = lax.axis_size(LON)
    core = lax.axis_index("core")
    low = lax.axis_index("y_lo") == 0
    flags = jnp.stack(
        [
            (lat_index == 0).astype(jnp.int32),
            (lat_index == lat_count - 1).astype(jnp.int32),
            core.astype(jnp.int32),
            low.astype(jnp.int32),
        ]
    )
    def shaped(*shape, dtype=BF16):
        return jax.ShapeDtypeStruct(shape, dtype)

    plane, side = shaped(ROWS, DEEP, LANES), shaped(SIDES // 2, variables * ROWS)
    weights, taps = shaped(9, DEEP, channels), (9, variables, channels)
    raw = (
        fields,
        recon_grad,
        jnp.swapaxes(enc_kernel, 2, 3).reshape(taps),
        gen_kernel.reshape(taps),
    )
    *raw, east, west = call(
        columns_kernel,
        tuple(shaped(*v.shape) for v in raw) + (side, side),
        10**7,
        [pltpu.SemaphoreType.DMA((4,))],
    )(in_specs=[FAR] * 4, out_specs=(FULL,) * 6)(
        *(pltpu.with_memory_space_constraint(v, pltpu.HBM) for v in raw)
    )
    turned = pltpu.VMEM((ROWS * DEEP, SIDES), F32)
    right = [(i, (i + 1) % lon_count) for i in range(lon_count)]
    left = [(b, a) for a, b in right]
    east = lax.ppermute(east, LON, right)
    west = lax.ppermute(west, LON, left)
    x, r, enc_rows, gen_rows = call(
        planes_kernel,
        (plane, plane, weights, weights),
        10**9,
        [pltpu.VMEM((ROWS * DEEP, LANES), F32)],
    )(in_specs=[FULL] * 4, out_specs=(FULL,) * 4)(*raw)
    enc_rows, gen_rows = (v.reshape(TAPS, channels) for v in (enc_rows, gen_rows))
    packet = shaped(4, SENT, LANES)
    pa, pb = call(rows_kernel, (packet, packet), 10**7, [turned])(
        in_specs=[FLAGS] + [FULL] * 4, out_specs=(FULL,) * 2
    )(flags, x, r, east, west)
    ahead, behind = great_circles(lat_count, lon_count)
    pa = lax.ppermute(pa, LAT + LON, ahead)
    pb = lax.ppermute(pb, LAT + LON, behind)
    we, gt = enc_rows.T, gen_rows.T
    sums, packed = (2, TAPS, channels), (2 * PACK, LANES)
    few = shaped(4, BAND, LANES)
    feat_mid, hid_mid, acc, fe, re = call(
        inner_kernel,
        (
            shaped(MID, channels, LANES),
            shaped(MID, channels, LANES),
            shaped(*sums, dtype=F32),
            few,
            few,
        ),
        9 * 10**9,
        [
            pltpu.VMEM((ROWS, BAND, LANES), BF16),
            pltpu.VMEM((ROWS, BAND, LANES), BF16),
            pltpu.VMEM((MID, channels, LANES), BF16),
            turned,
        ],
        16,
    )(in_specs=[FULL] * 6, out_specs=(FULL,) * 5)(x, r, east, west, we, gt)
    pair = shaped(2, channels, LANES)
    work = [pltpu.VMEM(sums[1:], F32), pltpu.VMEM((PACK + 8, channels), F32)]
    feat_edge, hid_edge, sent, lhs, rhs, poles = call(
        edge_kernel,
        (
            pair,
            pair,
            shaped(*packed),
            shaped(2, TAPS, 2 * LANES),
            shaped(2, channels, 2 * LANES),
            shaped(2, BAND, LANES),
        ),
        10**9,
        [pltpu.VMEM((2, BAND, LANES), BF16), pltpu.VMEM((2, BAND, LANES), BF16)] + work,
        16,
    )(in_specs=[FLAGS] + [FULL] * 7, out_specs=(FULL,) * 6)(
        flags, fe, re, pa, pb, we, gt, acc
    )
    kept = call(kept_kernel, shaped(*packed, dtype=F32), 10**9, work)(
        in_specs=[FLAGS] + [FULL] * 4, out_specs=FULL
    )(flags, acc, lhs, rhs, poles)
    half = (kept + swap_cores(sent).astype(F32)).astype(BF16)
    half, feat_edge, pa = lax.optimization_barrier((half, feat_edge, pa))
    halo, strip = call(
        beyond_kernel,
        (shaped(2, channels, LANES), shaped(channels, LANES)),
        10**9,
        [pltpu.VMEM((8, BAND, LANES), BF16), pltpu.VMEM((BAND, LANES), F32), turned],
    )(in_specs=[FLAGS] + [FULL] * 6, out_specs=(FULL,) * 2)(flags, x, east, west, pa, pb, we)
    rebuilt = call(
        rebuilt_kernel,
        shaped(variables, height, width),
        4 * 10**9,
        [
            pltpu.VMEM((ROWS + 2, TAPS, LANES), F32),
            pltpu.VMEM((DEEP, LANES), F32),
            pltpu.VMEM((DEEP * ROWS, LANES), F32),
        ],
        12,
    )(in_specs=[FULL] * 5, out_specs=FULL)(hid_mid, hid_edge, halo, strip, gen_rows)

    def turn(part, *earlier):
        half_channels = channels // 2
        return pl.pallas_call(
            functools.partial(turn_kernel, part),
            out_shape=shaped(channels, height, width),
            in_specs=[FULL] * 2 + [FAR] * len(earlier),
            out_specs=FAR,
            scratch_shapes=[
                pltpu.VMEM((half_channels * ROWS, LANES), F32),
                pltpu.VMEM((half_channels, height, width), BF16),
                pltpu.SemaphoreType.DMA,
            ],
            input_output_aliases={2: 0} if earlier else {},
            compiler_params=pltpu.CompilerParams(vmem_limit_bytes=8 << 20),
            cost_estimate=pl.CostEstimate(flops=10**9, bytes_accessed=10**6, transcendentals=0),
        )(feat_mid, feat_edge, *earlier)

    feat_grad = turn(0)
    faces, layers = lax.axis_size(FACE), lax.axis_size("z")
    piece = (2 * PACK // faces, LANES)

    def exchange(value, axes):
        return lax.all_to_all(value, axes, 0, 0, tiled=True)

    def total(pieces, copies):
        return call(total_kernel, jax.ShapeDtypeStruct((copies,) + piece, BF16), 10**7)(
            in_specs=[FULL], out_specs=FULL
        )(pieces)

    pieces = exchange(half.reshape((faces,) + piece), FACE)
    pieces, feat_grad, rebuilt = lax.optimization_barrier((pieces, feat_grad, rebuilt))
    pieces = exchange(total(pieces, layers), "z")
    own = exchange(total(pieces, faces), FACE).reshape(packed)
    own, feat_mid, feat_edge, feat_grad = lax.optimization_barrier(
        (own, feat_mid, feat_edge, feat_grad)
    )
    other = swap_cores(own)
    feat_grad = turn(1, feat_grad)
    norm = (height * lat_count * width * lon_count) ** -0.5
    grad = jax.ShapeDtypeStruct((9, variables, channels), F32)
    enc, gen = call(
        functools.partial(final_kernel, norm),
        (grad, grad),
        10**7,
        [
            pltpu.VMEM((2,) + packed, F32),
            pltpu.VMEM((2, 9, variables, channels), F32),
            pltpu.SemaphoreType.DMA((6,)),
        ],
    )(in_specs=[FLAGS, FULL, FULL], out_specs=(FAR, FAR))(flags, own, other)
    shape = (3, 3, variables, channels)
    return (rebuilt, feat_grad, jnp.swapaxes(enc.reshape(shape), 2, 3), gen.reshape(shape))


def solution(mesh):
    lat_count, lon_count = mesh.shape["lat"], mesh.shape["lon"]
    fine = Mesh(mesh.devices.reshape(lat_count // 2, 2, 2, lon_count // 4, 2), LAT + LON)
    return jax.shard_map(
        on_device,
        mesh=fine,
        in_specs=(P(None, LAT, LON), P(), P(), P(None, LAT, LON)),
        out_specs=(P(None, LAT, LON), P(None, LAT, LON), P(), P()),
        check_vma=False,
    )
```
